32 devices in a mesh: groups: 2 (over y), rows: 4 (over z), cols: 2 (over x), sub: 2 (over core).
Axes of the slice: x: 2, y: 2, z: 4, core: 2. Of those that a mesh axis runs over, the one named last changes fastest.
Arguments:
- latents: bfloat16 [16, 8, 768], P(('groups', 'rows', 'cols'), None, 'sub'), parts along dimension 0, may hold values from -36 to 36
- timestep: int32 [2], P('groups'), parts along dimension 0, may hold values from 0 to 999
- scan_order: int32 [8], replicated, may hold values from 0 to 7, each once
- modulation: bfloat16 [128, 3, 768], P(None, None, 'sub'), may hold values from -0.5 to 0.5
- input_proj: bfloat16 [768, 2, 1536], P(None, None, 'sub'), may hold values from -0.21875 to 0.21875
- conv_weight: float32 [4, 1536], P(None, 'sub'), may hold values from -3 to 3
- conv_bias: float32 [1536], P('sub'), may hold values from -2 to 2
- select_proj: bfloat16 [1536, 80], P('sub'), may hold values from -0.15625 to 0.15625
- step_proj: bfloat16 [48, 1536], P(None, 'sub'), may hold values from -0.875 to 0.875
- step_bias: float32 [1536], P('sub'), may hold values from -6 to -1
- decay_log: float32 [16, 1536], P(None, 'sub'), may hold values from 0 to 2.77
- skip_gain: float32 [1536], P('sub'), may hold values from 0.5 to 2
- output_proj: bfloat16 [1536, 768], P('sub'), may hold values from -0.15625 to 0.15625
Outputs:
- blended: bfloat16 [16, 8, 768], P(('groups', 'rows', 'cols'), None, 'sub'), parts along dimension 0
The draws below stay inside these ranges and needn't reach their ends.
There are 2 independent parts, one for each index of `groups`. The reference program is written for one: setup_inputs(seed, part) draws one part's arguments, and reference() takes and returns one part's arrays. A program takes and returns all parts, laid end to end along the dimension named above; an argument that names none is the same for every part. Nothing has to cross between parts.
All inputs are finite; a program needn't handle non-finite values.
Results may differ from the reference program's by a relative error of at most 0.0065.
Values may be sent and summed in bfloat16 or wider, within the bound.
No kernel may reach another device: no remote copies, remote signals or barrier semaphores. Data moves between devices by JAX's collectives and lax.ppermute only.
A program may use at most 64 MiB of HBM per device.

```python
import math
import jax
import jax.numpy as jnp
from jax import lax

D = 768
E = 1536
NS = 16
RANK = 48
KCONV = 4
TFREQ = 128
H = 8
W = 8
RP = 80


def draw_latents(key, part):
    key_token, key_channel, key_pattern = jax.random.split(key, 3)
    token_scale = jnp.exp(jax.random.uniform(key_token, (H, W, 1), minval=math.log(0.3), maxval=math.log(3.0)))
    channel_scale = jnp.exp(jax.random.uniform(key_channel, (D,), minval=math.log(0.3), maxval=math.log(3.0)))
    pattern = jnp.clip(jax.random.normal(key_pattern, (H, W, D)), -4.0, 4.0)
    return (token_scale * channel_scale * pattern).astype(jnp.bfloat16)


def shard_levels(stream_key, extent, cuts, smallest, largest):
    gain = 1.0
    for dim, blocks in cuts:
        heights = jax.random.uniform(jax.random.fold_in(jax.random.fold_in(stream_key, 6), dim), (blocks,), jnp.float32, smallest / len(cuts), largest / len(cuts))
        gain = gain * jnp.repeat(jnp.exp(heights), extent[dim] // blocks).reshape((-1,) + (1,) * (len(extent) - 1 - dim))
    return gain


def bell_draw(rng, shape, width, limit, cuts=(), held_as=jnp.bfloat16):
    loudness = shard_levels(rng, shape, cuts, -0.22, 0.18) if cuts else 1.0
    entries = jax.random.normal(rng, shape, jnp.float32) * width * loudness
    return jnp.minimum(jnp.maximum(entries, -limit), limit).astype(held_as)


def setup_inputs(seed: int = 0, part: int = 0) -> dict:
    keys = jax.random.split(jax.random.key(seed), 14)
    part_keys = jax.random.split(jax.random.fold_in(keys[13], part), 14)
    latents = draw_latents(jax.random.fold_in(jax.random.fold_in(keys[13], part), 71), part)
    timestep = jax.random.randint(part_keys[1], (1,), 0, 1000).astype(jnp.int32)
    scan_order = jax.random.permutation(keys[2], H).astype(jnp.int32)
    modulation = bell_draw(keys[3], (TFREQ, 3, D), TFREQ ** -0.5, 0.5, ((2, 2),))
    input_proj = bell_draw(keys[4], (D, 2, E), D ** -0.5, 0.21875, ((2, 2),))
    conv_weight = bell_draw(keys[5], (KCONV, E), KCONV ** -0.5, 3.0, ((1, 2),), jnp.float32)
    conv_bias = bell_draw(keys[6], (E,), 0.5, 2.0, ((0, 2),), jnp.float32)
    select_proj = bell_draw(keys[7], (E, RP), E ** -0.5, 0.15625, ((0, 2),))
    step_proj = bell_draw(keys[8], (RANK, E), RANK ** -0.5, 0.875, ((1, 2),))
    step_bias = jnp.clip(-6.0 + 5.0 * jax.random.uniform(keys[9], (E,), jnp.float32) ** shard_levels(keys[9], (E,), ((0, 2),), -0.2, 0.2), -6.0, -1.0)
    decay_log = jnp.clip(2.77 * jax.random.uniform(keys[10], (NS, E), jnp.float32) ** shard_levels(keys[10], (NS, E), ((1, 2),), -0.2, 0.2), 0.0, 2.77)
    skip_gain = jnp.clip(0.5 + 1.5 * jax.random.uniform(keys[11], (E,), jnp.float32) ** shard_levels(keys[11], (E,), ((0, 2),), -0.2, 0.2), 0.5, 2.0)
    output_proj = bell_draw(keys[12], (E, D), E ** -0.5, 0.15625, ((0, 2),))
    return {"latents": latents, "timestep": timestep, "scan_order": scan_order, "modulation": modulation, "input_proj": input_proj, "conv_weight": conv_weight, "conv_bias": conv_bias, "select_proj": select_proj, "step_proj": step_proj, "step_bias": step_bias, "decay_log": decay_log, "skip_gain": skip_gain, "output_proj": output_proj}


EPSILON = 1e-06

def embed_time(timestep, freq_count):
    halfway = freq_count // 2
    frequency = jnp.exp(-math.log(10000.0) * jnp.arange(halfway, dtype=jnp.float32) / halfway)
    angles = timestep.astype(jnp.float32)[0] * frequency
    return jnp.concatenate([jnp.cos(angles), jnp.sin(angles)]).astype(jnp.bfloat16)

def reference(latents, timestep, scan_order, modulation, input_proj, conv_weight, conv_bias, select_proj, step_proj, step_bias, decay_log, skip_gain, output_proj):
    time_embed = embed_time(timestep, TFREQ)
    mod_rows = jnp.dot(time_embed[None, :], modulation.reshape(TFREQ, 3 * D), preferred_element_type=jnp.float32)
    mod_rows = mod_rows.reshape(3, D).astype(jnp.bfloat16)
    scale_row = mod_rows[0].astype(jnp.float32)
    shift_row = mod_rows[1].astype(jnp.float32)
    gate_row = mod_rows[2].astype(jnp.float32)
    flat_in = input_proj.reshape(D, 2 * E)
    decay_rate = -jnp.exp(decay_log)
    column_block = 16 if W % 16 == 0 else W
    restore_index = jnp.zeros((H,), jnp.int32).at[scan_order].set(jnp.arange(H, dtype=jnp.int32))

    def columns(block):
        values = block.astype(jnp.float32)
        meansq = lax.optimization_barrier(jnp.mean(values * values, axis=-1, keepdims=True))
        normed = (values * lax.rsqrt(meansq + EPSILON) * (1.0 + scale_row) + shift_row).astype(jnp.bfloat16)
        projected = jnp.dot(normed.reshape(-1, D), flat_in, preferred_element_type=jnp.float32)
        projected = projected.astype(jnp.bfloat16).reshape(H, column_block, 2, E)
        seq_input = jnp.take(projected[:, :, 0], scan_order, axis=0).astype(jnp.float32)
        seq_gate = jnp.take(projected[:, :, 1], scan_order, axis=0).astype(jnp.float32)
        padded = jnp.pad(seq_input, ((KCONV - 1, 0), (0, 0), (0, 0)))
        conv_sum = conv_bias + jnp.zeros_like(seq_input)
        for offset in range(KCONV):
            conv_sum = conv_sum + conv_weight[offset] * padded[offset:offset + H]
        activated = jax.nn.silu(conv_sum).astype(jnp.bfloat16)
        selected = jnp.dot(activated.reshape(-1, E), select_proj, preferred_element_type=jnp.float32)
        step_low = selected[:, :RANK].astype(jnp.bfloat16)
        step_pre = jnp.dot(step_low, step_proj, preferred_element_type=jnp.float32)
        step_size = jax.nn.softplus(step_pre + step_bias).reshape(H, column_block, E)
        entry_coef = selected[:, RANK:RANK + NS].reshape(H, column_block, NS)
        exit_coef = selected[:, RANK + NS:].reshape(H, column_block, NS)
        act_float = activated.astype(jnp.float32)

        def advance(carried, pieces):
            step_now, act_now, entry_now, exit_now = pieces
            carried = jnp.exp(step_now[:, None, :] * decay_rate) * carried + (step_now * act_now)[:, None, :] * entry_now[:, :, None]
            output = lax.optimization_barrier(jnp.sum(exit_now[:, :, None] * carried, axis=1)) + skip_gain * act_now
            return (carried, output)
        initial = jnp.zeros((column_block, NS, E), jnp.float32)
        _, scanned = lax.scan(advance, initial, (step_size, act_float, entry_coef, exit_coef))
        gated = (scanned * jax.nn.silu(seq_gate)).astype(jnp.bfloat16)
        placed = jnp.take(gated, restore_index, axis=0)
        update = jnp.dot(placed.reshape(-1, E), output_proj, preferred_element_type=jnp.float32)
        update = update.astype(jnp.bfloat16).reshape(H, column_block, D)
        return (values + gate_row * update.astype(jnp.float32)).astype(jnp.bfloat16)
    stacked = latents.reshape(H, W // column_block, column_block, D).transpose(1, 0, 2, 3)
    blended = lax.map(columns, stacked)
    return blended.transpose(1, 0, 2, 3).reshape(H, W, D)
```

```python
import math

import jax
import jax.numpy as jnp
from jax import lax
from jax.experimental import pallas as pl
from jax.experimental.pallas import tpu as pltpu
from jax.sharding import PartitionSpec as P

NS = 16
RANK = 48


EPSILON = 1e-06


def embed_time(timestep, freq_count):
    halfway = freq_count // 2
    frequency = jnp.exp(-math.log(10000.0) * jnp.arange(halfway, dtype=jnp.float32) / halfway)
    angles = timestep.astype(jnp.float32)[0] * frequency
    return jnp.concatenate([jnp.cos(angles), jnp.sin(angles)]).astype(jnp.bfloat16)


def widen(latent_half, scale_shift):
    return (
        lax.all_gather(latent_half, "sub", axis=2, tiled=True),
        lax.all_gather(scale_shift, "sub", axis=1, tiled=True),
    )


def normalize(latent_full, scale_full):
    values = latent_full.astype(jnp.float32)
    meansq = jnp.mean(values * values, axis=-1, keepdims=True)
    scaled = values * lax.rsqrt(meansq + EPSILON)
    scale_row = scale_full[0].astype(jnp.float32)
    shift_row = scale_full[1].astype(jnp.float32)
    return (scaled * (1.0 + scale_row) + shift_row).astype(jnp.bfloat16)


def project_in(normed, input_proj):
    model_width = input_proj.shape[0]
    flat_weight = input_proj.reshape(model_width, -1)
    result = jnp.dot(
        normed.reshape(-1, model_width), flat_weight, preferred_element_type=jnp.float32
    )
    return result.astype(jnp.bfloat16).reshape(normed.shape[:-1] + (flat_weight.shape[1],))


def reorder(one_hot, sequence):
    return jnp.einsum("kh,hnc->knc", one_hot, sequence, preferred_element_type=jnp.float32).astype(
        jnp.bfloat16
    )


def restore(one_hot, sequence):
    return jnp.einsum("kh,knc->hnc", one_hot, sequence, preferred_element_type=jnp.float32).astype(
        jnp.bfloat16
    )


def scan_columns(
    projected, conv_weight, conv_bias, select_proj, step_proj, step_bias, decay_log, skip_gain
):
    height, item_count, doubled = projected.shape
    inner_width = doubled // 2
    seq_input = projected[..., :inner_width].astype(jnp.float32)
    seq_gate = projected[..., inner_width:].astype(jnp.float32)
    tap_count = conv_weight.shape[0]
    padded = jnp.pad(seq_input, ((tap_count - 1, 0), (0, 0), (0, 0)))
    conv_sum = conv_bias + jnp.zeros_like(seq_input)
    for offset in range(tap_count):
        conv_sum = conv_sum + conv_weight[offset] * padded[offset : offset + height]
    activated = jax.nn.silu(conv_sum).astype(jnp.bfloat16)
    flat_act = activated.reshape(height * item_count, inner_width)
    partial_value = lax.dot_general(
        select_proj, flat_act, (((0,), (1,)), ((), ())), preferred_element_type=jnp.float32
    )
    selected = lax.psum(partial_value, "sub")
    step_low = selected[:RANK].astype(jnp.bfloat16)
    step_pre = lax.dot_general(
        step_low, step_proj, (((0,), (0,)), ((), ())), preferred_element_type=jnp.float32
    )
    step_size = jax.nn.softplus(step_pre + step_bias).reshape(height, item_count, inner_width)
    entry_coef = selected[RANK : RANK + NS].T.reshape(height, item_count, NS)
    exit_coef = selected[RANK + NS :].T.reshape(height, item_count, NS)
    act_float = activated.astype(jnp.float32)
    decay_rate = -jnp.exp(decay_log)
    block_len = height // 16 if height % 16 == 0 else height
    blocks = height // block_len

    def split_blocks(tensor):
        return tensor.reshape((blocks, block_len) + tensor.shape[1:])

    def combine(earlier, latter):
        return (earlier[0] * latter[0], latter[0] * earlier[1] + latter[1])

    def advance(carried, pieces):
        step_blk, act_blk, entry_blk, exit_blk = pieces
        decays = jnp.exp(step_blk[:, :, None, :] * decay_rate)
        driving = (step_blk * act_blk)[:, :, None, :] * entry_blk[..., None]
        cum_decay, cum_drive = lax.associative_scan(combine, (decays, driving), axis=0)
        states = cum_drive + cum_decay * carried[None]
        output = jnp.sum(exit_blk[..., None] * states, axis=2) + skip_gain * act_blk
        return (states[-1], output)

    initial = jnp.zeros((item_count, NS, inner_width), jnp.float32)
    pieces_all = (
        split_blocks(step_size),
        split_blocks(act_float),
        split_blocks(entry_coef),
        split_blocks(exit_coef),
    )
    _, outputs = lax.scan(advance, initial, pieces_all)
    scanned = outputs.reshape(height, item_count, inner_width)
    return (scanned * jax.nn.silu(seq_gate)).astype(jnp.bfloat16)


def exchange_device(
    latents,
    timestep,
    scan_order,
    modulation,
    input_proj,
    conv_weight,
    conv_bias,
    select_proj,
    step_proj,
    step_bias,
    decay_log,
    skip_gain,
    output_proj,
):
    rows_dev, grid_width, half_model = latents.shape
    line_groups = lax.axis_size(("rows", "cols"))
    cols_dev = grid_width // line_groups
    height = rows_dev * line_groups
    inner_width = input_proj.shape[2]
    freq_count = modulation.shape[0]
    time_embed = embed_time(timestep, freq_count)
    mod_rows = jnp.dot(
        time_embed[None, :], modulation.reshape(freq_count, -1), preferred_element_type=jnp.float32
    )
    mod_rows = mod_rows.reshape(3, half_model).astype(jnp.bfloat16)
    scale_shift = mod_rows[:2]
    gate_row = mod_rows[2].astype(jnp.float32)
    one_hot = (scan_order[:, None] == jnp.arange(height, dtype=jnp.int32)[None, :]).astype(
        jnp.bfloat16
    )
    latent_full, scale_full = widen(latents, scale_shift)
    projected = project_in(normalize(latent_full, scale_full), input_proj)
    sectioned = projected.reshape(rows_dev, line_groups, cols_dev, 2 * inner_width)[None]
    received = lax.all_to_all(sectioned, ("rows", "cols"), split_axis=2, concat_axis=0, tiled=True)
    item_count = received.shape[3]
    ordered = reorder(one_hot, received.reshape(height, item_count, 2 * inner_width))
    gated = scan_columns(
        ordered, conv_weight, conv_bias, select_proj, step_proj, step_bias, decay_log, skip_gain
    )
    placed = restore(one_hot, gated)
    returned = lax.all_to_all(
        placed.reshape(line_groups, rows_dev, 1, item_count, inner_width),
        ("rows", "cols"),
        split_axis=0,
        concat_axis=2,
        tiled=True,
    )
    gathered = returned.reshape(rows_dev, line_groups, item_count, inner_width)
    partial_value = jnp.dot(
        gathered.reshape(rows_dev * grid_width, inner_width),
        output_proj,
        preferred_element_type=jnp.float32,
    )
    summed = lax.psum_scatter(
        partial_value.reshape(rows_dev, grid_width, -1).astype(jnp.bfloat16),
        "sub",
        scatter_dimension=2,
        tiled=True,
    )
    blended = latents.astype(jnp.float32) + gate_row * summed.astype(jnp.float32)
    return blended.astype(jnp.bfloat16)


LANES = 128
TOKEN_LIMIT = 256


def swap_cores(tensor):
    return lax.ppermute(tensor, "sub", [(0, 1), (1, 0)])


def sublane_copies(row, count):
    return jnp.broadcast_to(row, (count, row.shape[-1]))


def silu(values):
    return values * (1.0 / (1.0 + jnp.exp(-values)))


def softplus(values):
    return jnp.maximum(values, 0.0) + jnp.log1p(jnp.exp(-jnp.abs(values)))


def matmul(left, right):
    return jnp.dot(left, right, preferred_element_type=jnp.float32)


def rounded(values):
    return values.astype(jnp.bfloat16).astype(jnp.float32)


def block_kernel(
    order_ref,
    place_ref,
    mine_ref,
    other_ref,
    embed_ref,
    mod_mine,
    mod_other,
    in_mine,
    in_other,
    sel_mine,
    sel_other,
    step_mine,
    step_other,
    conv_mine,
    conv_other,
    bias_mine,
    bias_other,
    stepb_mine,
    stepb_other,
    decay_mine,
    decay_other,
    skip_mine,
    skip_other,
    out_mine,
    out_other,
    result_ref,
    normed_ref,
    act_ref,
    step_ref,
    drive_ref,
    entry_ref,
    exit_ref,
    sel_ref,
):
    height, width, half = mine_ref.shape
    inner = in_mine.shape[-1]
    taps = conv_mine.shape[0]
    own_row = place_ref[0]
    core = place_ref[1]
    on_first = core == 0

    embed = embed_ref[...]

    def mod_row(ref, index):
        return rounded(matmul(embed, ref[index]))[0:1]

    scale_mine, shift_mine = 1.0 + mod_row(mod_mine, 0), mod_row(mod_mine, 1)
    scale_other, shift_other = 1.0 + mod_row(mod_other, 0), mod_row(mod_other, 1)
    gate_row = mod_row(mod_mine, 2)

    def normalized(block):
        a = mine_ref[block].astype(jnp.float32)
        b = other_ref[block].astype(jnp.float32)
        total = jnp.sum(a * a, axis=-1, keepdims=True) + jnp.sum(b * b, axis=-1, keepdims=True)
        scaling = lax.rsqrt(total / (2.0 * half) + EPSILON)
        a = a * scaling * scale_mine + shift_mine
        b = b * scaling * scale_other + shift_other
        return jnp.where(on_first, a, b), jnp.where(on_first, b, a)

    position = jnp.int32(0)
    for k in range(height):
        row = order_ref[k]
        position = jnp.where(row == own_row, k, position)
        low, high = normalized(row ^ own_row)
        normed_ref[pl.ds(k * width, width), 0:half] = low
        normed_ref[pl.ds(k * width, width), half : 2 * half] = high
    normed = normed_ref[...].astype(jnp.bfloat16)
    own_normed = normed_ref[pl.ds(pl.multiple_of(position * width, width), width), :].astype(jnp.bfloat16)

    sides = (
        (in_mine, conv_mine, bias_mine, sel_mine, step_mine, stepb_mine, decay_mine, skip_mine, out_mine),
        (in_other, conv_other, bias_other, sel_other, step_other, stepb_other, decay_other, skip_other, out_other),
    )
    selected = None
    for side, (in_ref, conv_ref, bias_ref, sel, _, _, _, _, _) in enumerate(sides):
        seq = rounded(matmul(normed, in_ref[0]))
        taps_row = [conv_ref[i : i + 1, :] for i in range(taps)]
        pieces = []
        for k in range(height):
            total = jnp.broadcast_to(bias_ref[...], (width, inner))
            for i in range(taps):
                source = k - (taps - 1) + i
                if source >= 0:
                    total = total + taps_row[i] * seq[source * width : (source + 1) * width]
            pieces.append(silu(total))
        act = jnp.concatenate(pieces, axis=0).astype(jnp.bfloat16)
        act_ref[side] = act.astype(jnp.float32)
        part = lax.dot_general(act, sel[...], (((1,), (1,)), ((), ())), preferred_element_type=jnp.float32)
        selected = part if selected is None else selected + part
    sel_ref[...] = selected

    states = (selected.shape[1] - step_mine.shape[0]) // 2
    rank = step_mine.shape[0]
    low_rank = selected[:, :rank].astype(jnp.bfloat16)
    row_index = lax.broadcasted_iota(jnp.int32, (height * width, inner), 0)
    live = row_index < (position + 1) * width
    for side, (_, _, _, _, step_proj, stepb, _, _, _) in enumerate(sides):
        size = softplus(matmul(low_rank, step_proj[...]) + stepb[...])
        size = jnp.where(live, size, 0.0)
        step_ref[side] = size
        drive_ref[side] = size * act_ref[side]
    own_rows = pl.ds(pl.multiple_of(position * width, width), width)
    for n in range(states):
        column = selected[:, rank + n : rank + n + 1]
        entry_ref[n] = jnp.broadcast_to(column, (height * width, LANES))
    own_selected = sel_ref[own_rows, :]
    for n in range(states):
        column = own_selected[:, rank + states + n : rank + states + n + 1]
        exit_ref[n] = jnp.broadcast_to(column, (width, LANES))

    update = None
    for side, (in_ref, _, _, _, _, _, decay, skip, out_ref) in enumerate(sides):
        seq_gate = rounded(matmul(own_normed, in_ref[1]))
        rates = -jnp.exp(decay[...])
        outs = []
        for block in range(inner // LANES):
            lanes = slice(block * LANES, (block + 1) * LANES)
            carried = [None] * states
            rate = [sublane_copies(rates[n : n + 1, lanes], width) for n in range(states)]
            for k in range(height):
                rows = slice(k * width, (k + 1) * width)
                size = step_ref[side, rows, lanes]
                drive = drive_ref[side, rows, lanes]
                for n in range(states):
                    fresh = drive * entry_ref[n, rows, :]
                    if k:
                        fresh = jnp.exp(size * rate[n]) * carried[n] + fresh
                    carried[n] = fresh
            total = skip[:, lanes] * act_ref[side, own_rows, lanes]
            for n in range(states):
                total = total + exit_ref[n] * carried[n]
            outs.append(total)
        scanned = jnp.concatenate(outs, axis=1)
        gated = (scanned * silu(seq_gate)).astype(jnp.bfloat16)
        columns = pl.ds(pl.multiple_of(core * half, LANES), half)
        part = matmul(gated, out_ref[:, columns])
        update = part if update is None else update + part
    own_latent = mine_ref[0].astype(jnp.float32)
    result_ref[...] = (own_latent + gate_row * rounded(update)).astype(jnp.bfloat16)


def gather_device(
    latents,
    timestep,
    scan_order,
    modulation,
    input_proj,
    conv_weight,
    conv_bias,
    select_proj,
    step_proj,
    step_bias,
    decay_log,
    skip_gain,
    output_proj,
):
    _, width, half = latents.shape
    lines = lax.axis_size(("rows", "cols"))
    embed = embed_time(timestep, modulation.shape[0])
    gathered = latents
    reach = 1
    while reach < lines:
        pairs = [(i, i ^ reach) for i in range(lines)]
        gathered = jnp.concatenate([gathered, lax.ppermute(gathered, ("rows", "cols"), pairs)], 0)
        reach *= 2
    other = swap_cores(gathered)
    place = jnp.stack([lax.axis_index(("rows", "cols")), lax.axis_index("sub")]).astype(jnp.int32)
    locals_ = (
        modulation.transpose(1, 0, 2),
        input_proj.transpose(1, 0, 2),
        select_proj.T,
        step_proj,
        conv_weight,
        conv_bias[None],
        step_bias[None],
        decay_log,
        skip_gain[None],
        output_proj,
    )
    paired = []
    for tensor in locals_:
        paired += [tensor, swap_cores(tensor)]
    height, inner = lines, input_proj.shape[-1]
    tokens, states = height * width, decay_log.shape[0]
    smem = pl.BlockSpec(memory_space=pltpu.SMEM)
    vmem = pl.BlockSpec(memory_space=pltpu.VMEM)
    embed_rows = jnp.broadcast_to(embed[None], (16, embed.shape[0]))
    result = pl.pallas_call(
        block_kernel,
        out_shape=jax.ShapeDtypeStruct((width, half), jnp.bfloat16),
        in_specs=[smem, smem] + [vmem] * (3 + len(paired)),
        out_specs=vmem,
        scratch_shapes=[
            pltpu.VMEM((tokens, 2 * half), jnp.float32),
            pltpu.VMEM((2, tokens, inner), jnp.float32),
            pltpu.VMEM((2, tokens, inner), jnp.float32),
            pltpu.VMEM((2, tokens, inner), jnp.float32),
            pltpu.VMEM((states, tokens, LANES), jnp.float32),
            pltpu.VMEM((states, width, LANES), jnp.float32),
            pltpu.VMEM((tokens, select_proj.shape[1]), jnp.float32),
        ],
        compiler_params=pltpu.CompilerParams(vmem_limit_bytes=24 << 20),
        name="scan_block",
    )(scan_order, place, gathered, other, embed_rows, *paired)
    return result[None]


def on_device(latents, *others):
    rows_dev, grid_width, half = latents.shape
    lines = lax.axis_size(("rows", "cols"))
    small = rows_dev == 1 and lines & (lines - 1) == 0 and lines * grid_width <= TOKEN_LIMIT
    tiled = grid_width % 8 == 0 and half % LANES == 0 and lax.axis_size("sub") == 2
    run = gather_device if small and tiled else exchange_device
    return run(latents, *others)


def solution(mesh):
    placed = (
        P(("groups", "rows", "cols"), None, "sub"),
        P("groups"),
        P(),
        P(None, None, "sub"),
        P(None, None, "sub"),
        P(None, "sub"),
        P("sub"),
        P("sub", None),
        P(None, "sub"),
        P("sub"),
        P(None, "sub"),
        P("sub"),
        P("sub", None),
    )
    return jax.shard_map(
        on_device,
        mesh=mesh,
        in_specs=placed,
        out_specs=P(("groups", "rows", "cols"), None, "sub"),
        check_vma=False,
    )
```

```python
import functools
import math

import jax
import jax.numpy as jnp
from jax import lax
from jax.experimental import pallas as pl
from jax.experimental.pallas import tpu as pltpu
from jax.sharding import PartitionSpec as P


NS = 16
RANK = 48


EPSILON = 1e-06


def embed_time(timestep, freq_count):
    halfway = freq_count // 2
    frequency = jnp.exp(-math.log(10000.0) * jnp.arange(halfway, dtype=jnp.float32) / halfway)
    angles = timestep.astype(jnp.float32)[0] * frequency
    return jnp.concatenate([jnp.cos(angles), jnp.sin(angles)]).astype(jnp.bfloat16)


def widen(latent_half, scale_shift):
    return (
        lax.all_gather(latent_half, "sub", axis=2, tiled=True),
        lax.all_gather(scale_shift, "sub", axis=1, tiled=True),
    )


def normalize(latent_full, scale_full):
    values = latent_full.astype(jnp.float32)
    meansq = jnp.mean(values * values, axis=-1, keepdims=True)
    scaled = values * lax.rsqrt(meansq + EPSILON)
    scale_row = scale_full[0].astype(jnp.float32)
    shift_row = scale_full[1].astype(jnp.float32)
    return (scaled * (1.0 + scale_row) + shift_row).astype(jnp.bfloat16)


def project_in(normed, input_proj):
    model_width = input_proj.shape[0]
    flat_weight = input_proj.reshape(model_width, -1)
    result = jnp.dot(
        normed.reshape(-1, model_width), flat_weight, preferred_element_type=jnp.float32
    )
    return result.astype(jnp.bfloat16).reshape(normed.shape[:-1] + (flat_weight.shape[1],))


def reorder(one_hot, sequence):
    return jnp.einsum("kh,hnc->knc", one_hot, sequence, preferred_element_type=jnp.float32).astype(
        jnp.bfloat16
    )


def restore(one_hot, sequence):
    return jnp.einsum("kh,knc->hnc", one_hot, sequence, preferred_element_type=jnp.float32).astype(
        jnp.bfloat16
    )


def scan_columns(
    projected, conv_weight, conv_bias, select_proj, step_proj, step_bias, decay_log, skip_gain
):
    height, item_count, doubled = projected.shape
    inner_width = doubled // 2
    seq_input = projected[..., :inner_width].astype(jnp.float32)
    seq_gate = projected[..., inner_width:].astype(jnp.float32)
    tap_count = conv_weight.shape[0]
    padded = jnp.pad(seq_input, ((tap_count - 1, 0), (0, 0), (0, 0)))
    conv_sum = conv_bias + jnp.zeros_like(seq_input)
    for offset in range(tap_count):
        conv_sum = conv_sum + conv_weight[offset] * padded[offset : offset + height]
    activated = jax.nn.silu(conv_sum).astype(jnp.bfloat16)
    flat_act = activated.reshape(height * item_count, inner_width)
    partial_value = lax.dot_general(
        select_proj, flat_act, (((0,), (1,)), ((), ())), preferred_element_type=jnp.float32
    )
    selected = lax.psum(partial_value, "sub")
    step_low = selected[:RANK].astype(jnp.bfloat16)
    step_pre = lax.dot_general(
        step_low, step_proj, (((0,), (0,)), ((), ())), preferred_element_type=jnp.float32
    )
    step_size = jax.nn.softplus(step_pre + step_bias).reshape(height, item_count, inner_width)
    entry_coef = selected[RANK : RANK + NS].T.reshape(height, item_count, NS)
    exit_coef = selected[RANK + NS :].T.reshape(height, item_count, NS)
    act_float = activated.astype(jnp.float32)
    decay_rate = -jnp.exp(decay_log)
    block_len = height // 16 if height % 16 == 0 else height
    blocks = height // block_len

    def split_blocks(tensor):
        return tensor.reshape((blocks, block_len) + tensor.shape[1:])

    def combine(earlier, latter):
        return (earlier[0] * latter[0], latter[0] * earlier[1] + latter[1])

    def advance(carried, pieces):
        step_blk, act_blk, entry_blk, exit_blk = pieces
        decays = jnp.exp(step_blk[:, :, None, :] * decay_rate)
        driving = (step_blk * act_blk)[:, :, None, :] * entry_blk[..., None]
        cum_decay, cum_drive = lax.associative_scan(combine, (decays, driving), axis=0)
        states = cum_drive + cum_decay * carried[None]
        output = jnp.sum(exit_blk[..., None] * states, axis=2) + skip_gain * act_blk
        return (states[-1], output)

    initial = jnp.zeros((item_count, NS, inner_width), jnp.float32)
    pieces_all = (
        split_blocks(step_size),
        split_blocks(act_float),
        split_blocks(entry_coef),
        split_blocks(exit_coef),
    )
    _, outputs = lax.scan(advance, initial, pieces_all)
    scanned = outputs.reshape(height, item_count, inner_width)
    return (scanned * jax.nn.silu(seq_gate)).astype(jnp.bfloat16)


def exchange_device(
    latents,
    timestep,
    scan_order,
    modulation,
    input_proj,
    conv_weight,
    conv_bias,
    select_proj,
    step_proj,
    step_bias,
    decay_log,
    skip_gain,
    output_proj,
):
    rows_dev, grid_width, half_model = latents.shape
    line_groups = lax.axis_size(("rows", "cols"))
    cols_dev = grid_width // line_groups
    height = rows_dev * line_groups
    inner_width = input_proj.shape[2]
    freq_count = modulation.shape[0]
    time_embed = embed_time(timestep, freq_count)
    mod_rows = jnp.dot(
        time_embed[None, :], modulation.reshape(freq_count, -1), preferred_element_type=jnp.float32
    )
    mod_rows = mod_rows.reshape(3, half_model).astype(jnp.bfloat16)
    scale_shift = mod_rows[:2]
    gate_row = mod_rows[2].astype(jnp.float32)
    one_hot = (scan_order[:, None] == jnp.arange(height, dtype=jnp.int32)[None, :]).astype(
        jnp.bfloat16
    )
    latent_full, scale_full = widen(latents, scale_shift)
    projected = project_in(normalize(latent_full, scale_full), input_proj)
    sectioned = projected.reshape(rows_dev, line_groups, cols_dev, 2 * inner_width)[None]
    received = lax.all_to_all(sectioned, ("rows", "cols"), split_axis=2, concat_axis=0, tiled=True)
    item_count = received.shape[3]
    ordered = reorder(one_hot, received.reshape(height, item_count, 2 * inner_width))
    gated = scan_columns(
        ordered, conv_weight, conv_bias, select_proj, step_proj, step_bias, decay_log, skip_gain
    )
    placed = restore(one_hot, gated)
    returned = lax.all_to_all(
        placed.reshape(line_groups, rows_dev, 1, item_count, inner_width),
        ("rows", "cols"),
        split_axis=0,
        concat_axis=2,
        tiled=True,
    )
    gathered = returned.reshape(rows_dev, line_groups, item_count, inner_width)
    partial_value = jnp.dot(
        gathered.reshape(rows_dev * grid_width, inner_width),
        output_proj,
        preferred_element_type=jnp.float32,
    )
    summed = lax.psum_scatter(
        partial_value.reshape(rows_dev, grid_width, -1).astype(jnp.bfloat16),
        "sub",
        scatter_dimension=2,
        tiled=True,
    )
    blended = latents.astype(jnp.float32) + gate_row * summed.astype(jnp.float32)
    return blended.astype(jnp.bfloat16)


LANES = 128
TOKEN_LIMIT = 256
LOG2_E = math.log2(math.e)


def swap_cores(tensor):
    return lax.ppermute(tensor, "sub", [(0, 1), (1, 0)])


def silu(values):
    half = 0.5 * values
    return half + half * jnp.tanh(half)


def softplus(values):
    return jnp.maximum(values, 0.0) + jnp.log(1.0 + jnp.exp(-jnp.abs(values)))


def matmul(left, right):
    return jnp.dot(left, right, preferred_element_type=jnp.float32)


def rounded(values):
    return values.astype(jnp.bfloat16).astype(jnp.float32)


def pack_kernel(sel_ref, step_ref, mod_ref, conv_ref, bias_ref, stepb_ref, skip_ref, decay_ref, narrow_ref, wide_ref):
    coefs, rank, taps = sel_ref.shape[0], step_ref.shape[0], conv_ref.shape[0]
    half = mod_ref.shape[-1]
    narrow_ref[:coefs] = sel_ref[...]
    narrow_ref[coefs : coefs + rank] = step_ref[...]
    narrow_ref[coefs + rank :, :half] = mod_ref[0]
    narrow_ref[coefs + rank :, half:] = mod_ref[1]
    wide_ref[:taps] = conv_ref[...]
    for i, ref in enumerate((bias_ref, stepb_ref, skip_ref, skip_ref)):
        wide_ref[taps + i : taps + i + 1] = ref[...]
    wide_ref[taps + 4 :] = -LOG2_E * jnp.exp(decay_ref[...])


def prepare_kernel(lead, order_ref, embed_ref, mod_ref, narrow_ref, pick_ref, live_ref, rows_ref):
    height = order_ref.shape[0]
    tokens = pick_ref.shape[0]
    width, half = tokens // height, mod_ref.shape[-1]
    own_row = lax.axis_index("rows") * lax.axis_size("cols") + lax.axis_index("cols")
    position = jnp.int32(0)
    for k in range(height):
        position = jnp.where(order_ref[k] == own_row, k, position)
    slot = lax.broadcasted_iota(jnp.int32, (width, tokens), 0)
    column = lax.broadcasted_iota(jnp.int32, (width, tokens), 1)
    picks = []
    for j in range(height):
        block = order_ref[jnp.maximum(position - j, 0)] ^ own_row
        target = jnp.where(position >= j, block * width, -width) + slot
        picks.append(jnp.where(column == target, 1.0, 0.0))
        live_ref[j * width : (j + 1) * width] = jnp.full((width, LANES), jnp.where(position >= j, 1.0, 0.0))
    pick_ref[...] = jnp.concatenate(picks, axis=0).astype(jnp.bfloat16)
    embed = jnp.broadcast_to(embed_ref[...], (16, embed_ref.shape[1]))
    weights = (mod_ref[0], mod_ref[1], narrow_ref[lead:, :half], narrow_ref[lead:, half:], mod_ref[2])
    for i, weight in enumerate(weights):
        row = rounded(matmul(embed, weight))[:1]
        rows_ref[i : i + 1] = 1.0 + row if i in (0, 2) else row


def block_kernel(
    taps,
    states,
    rank,
    pick_ref,
    live_ref,
    rows_ref,
    mine_ref,
    other_ref,
    in_mine,
    in_other,
    narrow_mine,
    narrow_other,
    wide_mine,
    wide_other,
    out_mine,
    out_other,
    result_ref,
    act_ref,
    pre_ref,
    weight_ref,
):
    height, width, half = mine_ref.shape
    tokens = height * width
    inner = in_mine.shape[-1]
    core = lax.axis_index("sub")
    on_first = core == 0
    coefs = rank + 2 * states
    scale_mine, shift_mine, scale_other, shift_other, gate_row = [rows_ref[i : i + 1] for i in range(5)]

    pick = pick_ref[...]
    first = matmul(pick, mine_ref[...].reshape(tokens, half))
    second = matmul(pick, other_ref[...].reshape(tokens, half))
    total = jnp.sum(first * first + second * second, axis=-1, keepdims=True)
    scaling = lax.rsqrt(total / (2.0 * half) + EPSILON)
    live = live_ref[...]
    live_half = jnp.concatenate([live] * (half // LANES), axis=1)
    first = (first * scaling * scale_mine + shift_mine) * live_half
    second = (second * scaling * scale_other + shift_other) * live_half
    low = jnp.where(on_first, first, second)
    high = jnp.where(on_first, second, first)
    normed = jnp.concatenate([low, high], axis=1).astype(jnp.bfloat16)
    own_normed = normed[:width]

    sides = ((in_mine, narrow_mine, wide_mine, out_mine), (in_other, narrow_other, wide_other, out_other))
    selected = None
    for side, (in_ref, narrow, wide, _) in enumerate(sides):
        seq = rounded(matmul(normed, in_ref[0]))
        pieces = []
        for j in range(height):
            mixed = wide[taps : taps + 1, :]
            for back in range(min(taps, height - j)):
                tap = taps - 1 - back
                mixed = mixed + wide[tap : tap + 1, :] * seq[(j + back) * width : (j + back + 1) * width]
            pieces.append(silu(mixed))
        act = jnp.concatenate(pieces, axis=0).astype(jnp.bfloat16)
        act_ref[side] = act.astype(jnp.float32)
        part = lax.dot_general(
            act, narrow[:coefs, :], (((1,), (1,)), ((), ())), preferred_element_type=jnp.float32
        )
        selected = part if selected is None else selected + part

    low_rank = selected[:, :rank].astype(jnp.bfloat16)
    for side, (_, narrow, _, _) in enumerate(sides):
        pre_ref[side] = matmul(low_rank, narrow[coefs : coefs + rank, :])
    own_exit = selected[:width, rank + states :]
    for j in range(height):
        product = selected[j * width : (j + 1) * width, rank : rank + states] * own_exit
        for n in range(states):
            weight_ref[j, n] = jnp.broadcast_to(product[:, n : n + 1], (width, LANES))

    update = None
    columns = pl.ds(pl.multiple_of(core * half, LANES), half)
    for side, (in_ref, _, wide, out_ref) in enumerate(sides):
        gate = silu(rounded(matmul(own_normed, in_ref[1])))
        rates = wide[taps + 4 :, :]
        step_bias, skip = wide[taps + 1 : taps + 2, :], wide[taps + 2 : taps + 3, :]
        outs = []
        for block in range(inner // LANES):
            lanes = slice(block * LANES, (block + 1) * LANES)
            size = softplus(pre_ref[side, :, lanes] + step_bias[:, lanes])
            act = act_ref[side, :, lanes]
            drive = size * act * live
            rate = [jnp.broadcast_to(rates[n : n + 1, lanes], (width, LANES)) for n in range(states)]
            scanned = skip[:, lanes] * act[:width]
            elapsed = None
            for j in range(height):
                rows = slice(j * width, (j + 1) * width)
                mixed = None
                for n in range(states):
                    term = weight_ref[j, n]
                    if j:
                        term = jnp.exp2(elapsed * rate[n]) * term
                    mixed = term if mixed is None else mixed + term
                scanned = scanned + drive[rows] * mixed
                elapsed = size[rows] if elapsed is None else elapsed + size[rows]
            outs.append((scanned * gate[:, lanes]).astype(jnp.bfloat16))
        part = matmul(jnp.concatenate(outs, axis=1), out_ref[:, columns])
        update = part if update is None else update + part
    own_latent = mine_ref[0].astype(jnp.float32)
    result_ref[...] = (own_latent + gate_row * rounded(update)).astype(jnp.bfloat16)


def gather_device(
    latents,
    timestep,
    scan_order,
    modulation,
    input_proj,
    conv_weight,
    conv_bias,
    select_proj,
    step_proj,
    step_bias,
    decay_log,
    skip_gain,
    output_proj,
):
    _, width, half = latents.shape
    lines = lax.axis_size(("rows", "cols"))
    inner, states = input_proj.shape[-1], decay_log.shape[0]
    taps, rank = conv_weight.shape[0], step_proj.shape[0]
    tokens = lines * width
    freq_count = modulation.shape[0]
    vmem = pl.BlockSpec(memory_space=pltpu.VMEM)
    smem = pl.BlockSpec(memory_space=pltpu.SMEM)
    by_row = modulation.transpose(1, 0, 2)
    coefs = select_proj.shape[1]
    packed = pl.pallas_call(
        pack_kernel,
        out_shape=(
            jax.ShapeDtypeStruct((coefs + rank + freq_count, inner), jnp.bfloat16),
            jax.ShapeDtypeStruct((taps + 4 + states, inner), jnp.float32),
        ),
        in_specs=[vmem] * 8,
        out_specs=(vmem, vmem),
        compiler_params=pltpu.CompilerParams(vmem_limit_bytes=8 << 20),
        name="pack_small",
    )
    gathered = latents
    reach = 1
    model = input_proj.shape[0]
    cut = model // 3 * 2 if model % 3 == 0 else model // 2
    parts = [input_proj[part].transpose(1, 0, 2) for part in (slice(0, cut), slice(cut, None))]
    into = jnp.concatenate(parts, axis=1)
    out_other = swap_cores(output_proj)
    while reach < lines:
        pairs = [(i, i ^ reach) for i in range(lines)]
        arrived = lax.ppermute(gathered, ("rows", "cols"), pairs)
        gathered = jnp.concatenate([gathered, arrived], 0)
        reach = 2 * reach
    other = swap_cores(gathered)
    into_other = swap_cores(into)
    narrow, wide = packed(
        select_proj.T, step_proj, by_row, conv_weight, conv_bias[None], step_bias[None], skip_gain[None], decay_log
    )
    narrow_other = swap_cores(narrow)
    wide_other = swap_cores(wide)
    embed = embed_time(timestep, freq_count)
    pick, live, rows = pl.pallas_call(
        functools.partial(prepare_kernel, coefs + rank),
        out_shape=(
            jax.ShapeDtypeStruct((tokens, tokens), jnp.bfloat16),
            jax.ShapeDtypeStruct((tokens, LANES), jnp.float32),
            jax.ShapeDtypeStruct((8, half), jnp.float32),
        ),
        in_specs=[smem, vmem, vmem, vmem],
        out_specs=(vmem, vmem, vmem),
        compiler_params=pltpu.CompilerParams(vmem_limit_bytes=8 << 20),
        name="prepare",
    )(scan_order, embed[None], by_row, narrow_other)
    operands = (
        pick,
        live,
        rows,
        gathered,
        other,
        into,
        into_other,
        narrow,
        narrow_other,
        wide,
        wide_other,
        output_proj,
        out_other,
    )
    result = pl.pallas_call(
        functools.partial(block_kernel, taps, states, rank),
        out_shape=jax.ShapeDtypeStruct((width, half), jnp.bfloat16),
        in_specs=[vmem] * len(operands),
        out_specs=vmem,
        scratch_shapes=[
            pltpu.VMEM((2, tokens, inner), jnp.float32),
            pltpu.VMEM((2, tokens, inner), jnp.float32),
            pltpu.VMEM((lines, states, width, LANES), jnp.float32),
        ],
        compiler_params=pltpu.CompilerParams(vmem_limit_bytes=16 << 20),
        name="scan_block",
    )(*operands)
    return result[None]


def on_device(latents, *others):
    rows_dev, grid_width, half = latents.shape
    lines = lax.axis_size(("rows", "cols"))
    small = rows_dev == 1 and lines & (lines - 1) == 0 and lines * grid_width <= TOKEN_LIMIT
    tiled = grid_width % 8 == 0 and half % LANES == 0 and lax.axis_size("sub") == 2
    run = gather_device if small and tiled else exchange_device
    return run(latents, *others)


def solution(mesh):
    placed = (
        P(("groups", "rows", "cols"), None, "sub"),
        P("groups"),
        P(),
        P(None, None, "sub"),
        P(None, None, "sub"),
        P(None, "sub"),
        P("sub"),
        P("sub", None),
        P(None, "sub"),
        P("sub"),
        P(None, "sub"),
        P("sub"),
        P("sub", None),
    )
    return jax.shard_map(
        on_device,
        mesh=mesh,
        in_specs=placed,
        out_specs=P(("groups", "rows", "cols"), None, "sub"),
        check_vma=False,
    )
```

```python
import functools
import math

import jax
import jax.numpy as jnp
from jax import lax
from jax.experimental import pallas as pl
from jax.experimental.pallas import tpu as pltpu
from jax.sharding import PartitionSpec as P


NS = 16
RANK = 48


EPSILON = 1e-06


def embed_time(timestep, freq_count):
    halfway = freq_count // 2
    frequency = jnp.exp(-math.log(10000.0) * jnp.arange(halfway, dtype=jnp.float32) / halfway)
    angles = timestep.astype(jnp.float32)[0] * frequency
    return jnp.concatenate([jnp.cos(angles), jnp.sin(angles)]).astype(jnp.bfloat16)


def widen(latent_half, scale_shift):
    return (
        lax.all_gather(latent_half, "sub", axis=2, tiled=True),
        lax.all_gather(scale_shift, "sub", axis=1, tiled=True),
    )


def normalize(latent_full, scale_full):
    values = latent_full.astype(jnp.float32)
    meansq = jnp.mean(values * values, axis=-1, keepdims=True)
    scaled = values * lax.rsqrt(meansq + EPSILON)
    scale_row = scale_full[0].astype(jnp.float32)
    shift_row = scale_full[1].astype(jnp.float32)
    return (scaled * (1.0 + scale_row) + shift_row).astype(jnp.bfloat16)


def project_in(normed, input_proj):
    model_width = input_proj.shape[0]
    flat_weight = input_proj.reshape(model_width, -1)
    result = jnp.dot(
        normed.reshape(-1, model_width), flat_weight, preferred_element_type=jnp.float32
    )
    return result.astype(jnp.bfloat16).reshape(normed.shape[:-1] + (flat_weight.shape[1],))


def reorder(one_hot, sequence):
    return jnp.einsum("kh,hnc->knc", one_hot, sequence, preferred_element_type=jnp.float32).astype(
        jnp.bfloat16
    )


def restore(one_hot, sequence):
    return jnp.einsum("kh,knc->hnc", one_hot, sequence, preferred_element_type=jnp.float32).astype(
        jnp.bfloat16
    )


def scan_columns(
    projected, conv_weight, conv_bias, select_proj, step_proj, step_bias, decay_log, skip_gain
):
    height, item_count, doubled = projected.shape
    inner_width = doubled // 2
    seq_input = projected[..., :inner_width].astype(jnp.float32)
    seq_gate = projected[..., inner_width:].astype(jnp.float32)
    tap_count = conv_weight.shape[0]
    padded = jnp.pad(seq_input, ((tap_count - 1, 0), (0, 0), (0, 0)))
    conv_sum = conv_bias + jnp.zeros_like(seq_input)
    for offset in range(tap_count):
        conv_sum = conv_sum + conv_weight[offset] * padded[offset : offset + height]
    activated = jax.nn.silu(conv_sum).astype(jnp.bfloat16)
    flat_act = activated.reshape(height * item_count, inner_width)
    partial_value = lax.dot_general(
        select_proj, flat_act, (((0,), (1,)), ((), ())), preferred_element_type=jnp.float32
    )
    selected = lax.psum(partial_value, "sub")
    step_low = selected[:RANK].astype(jnp.bfloat16)
    step_pre = lax.dot_general(
        step_low, step_proj, (((0,), (0,)), ((), ())), preferred_element_type=jnp.float32
    )
    step_size = jax.nn.softplus(step_pre + step_bias).reshape(height, item_count, inner_width)
    entry_coef = selected[RANK : RANK + NS].T.reshape(height, item_count, NS)
    exit_coef = selected[RANK + NS :].T.reshape(height, item_count, NS)
    act_float = activated.astype(jnp.float32)
    decay_rate = -jnp.exp(decay_log)
    block_len = height // 16 if height % 16 == 0 else height
    blocks = height // block_len

    def split_blocks(tensor):
        return tensor.reshape((blocks, block_len) + tensor.shape[1:])

    def combine(earlier, latter):
        return (earlier[0] * latter[0], latter[0] * earlier[1] + latter[1])

    def advance(carried, pieces):
        step_blk, act_blk, entry_blk, exit_blk = pieces
        decays = jnp.exp(step_blk[:, :, None, :] * decay_rate)
        driving = (step_blk * act_blk)[:, :, None, :] * entry_blk[..., None]
        cum_decay, cum_drive = lax.associative_scan(combine, (decays, driving), axis=0)
        states = cum_drive + cum_decay * carried[None]
        output = jnp.sum(exit_blk[..., None] * states, axis=2) + skip_gain * act_blk
        return (states[-1], output)

    initial = jnp.zeros((item_count, NS, inner_width), jnp.float32)
    pieces_all = (
        split_blocks(step_size),
        split_blocks(act_float),
        split_blocks(entry_coef),
        split_blocks(exit_coef),
    )
    _, outputs = lax.scan(advance, initial, pieces_all)
    scanned = outputs.reshape(height, item_count, inner_width)
    return (scanned * jax.nn.silu(seq_gate)).astype(jnp.bfloat16)


def exchange_device(
    latents,
    timestep,
    scan_order,
    modulation,
    input_proj,
    conv_weight,
    conv_bias,
    select_proj,
    step_proj,
    step_bias,
    decay_log,
    skip_gain,
    output_proj,
):
    rows_dev, grid_width, half_model = latents.shape
    line_groups = lax.axis_size(("rows", "cols"))
    cols_dev = grid_width // line_groups
    height = rows_dev * line_groups
    inner_width = input_proj.shape[2]
    freq_count = modulation.shape[0]
    time_embed = embed_time(timestep, freq_count)
    mod_rows = jnp.dot(
        time_embed[None, :], modulation.reshape(freq_count, -1), preferred_element_type=jnp.float32
    )
    mod_rows = mod_rows.reshape(3, half_model).astype(jnp.bfloat16)
    scale_shift = mod_rows[:2]
    gate_row = mod_rows[2].astype(jnp.float32)
    one_hot = (scan_order[:, None] == jnp.arange(height, dtype=jnp.int32)[None, :]).astype(
        jnp.bfloat16
    )
    latent_full, scale_full = widen(latents, scale_shift)
    projected = project_in(normalize(latent_full, scale_full), input_proj)
    sectioned = projected.reshape(rows_dev, line_groups, cols_dev, 2 * inner_width)[None]
    received = lax.all_to_all(sectioned, ("rows", "cols"), split_axis=2, concat_axis=0, tiled=True)
    item_count = received.shape[3]
    ordered = reorder(one_hot, received.reshape(height, item_count, 2 * inner_width))
    gated = scan_columns(
        ordered, conv_weight, conv_bias, select_proj, step_proj, step_bias, decay_log, skip_gain
    )
    placed = restore(one_hot, gated)
    returned = lax.all_to_all(
        placed.reshape(line_groups, rows_dev, 1, item_count, inner_width),
        ("rows", "cols"),
        split_axis=0,
        concat_axis=2,
        tiled=True,
    )
    gathered = returned.reshape(rows_dev, line_groups, item_count, inner_width)
    partial_value = jnp.dot(
        gathered.reshape(rows_dev * grid_width, inner_width),
        output_proj,
        preferred_element_type=jnp.float32,
    )
    summed = lax.psum_scatter(
        partial_value.reshape(rows_dev, grid_width, -1).astype(jnp.bfloat16),
        "sub",
        scatter_dimension=2,
        tiled=True,
    )
    blended = latents.astype(jnp.float32) + gate_row * summed.astype(jnp.float32)
    return blended.astype(jnp.bfloat16)


LANES = 128
TOKEN_LIMIT = 256
LOG2_E = math.log2(math.e)


def swap_cores(tensor):
    return lax.ppermute(tensor, "sub", [(0, 1), (1, 0)])


def silu(values):
    half = 0.5 * values
    return half + half * jnp.tanh(half)


def softplus(values):
    return jnp.maximum(values, 0.0) + jnp.log(1.0 + jnp.exp(-jnp.abs(values)))


def matmul(left, right):
    return jnp.dot(left, right, preferred_element_type=jnp.float32)


def rounded(values):
    return values.astype(jnp.bfloat16).astype(jnp.float32)


def fetch_kernel(
    sel_ref,
    step_ref,
    mod_ref,
    into_ref,
    conv_ref,
    decay_ref,
    bias_ref,
    stepb_ref,
    skip_ref,
    latent_ref,
    out_ref,
    narrow_ref,
    wide_ref,
    held_ref,
    own_ref,
    send_ref,
    conv_buf,
    decay_buf,
    vector_bufs,
    sems,
):
    coefs, rank, taps = sel_ref.shape[0], step_ref.shape[0], conv_ref.shape[0]
    half = mod_ref.shape[-1]
    vectors = (bias_ref, stepb_ref, skip_ref)
    moves = [
        (conv_ref, conv_buf),
        (decay_ref, decay_buf),
        *((ref, vector_bufs[i]) for i, ref in enumerate(vectors)),
        (sel_ref, narrow_ref.at[:coefs]),
        (step_ref, narrow_ref.at[coefs : coefs + rank]),
        (mod_ref.at[0], narrow_ref.at[coefs + rank :, :half]),
        (mod_ref.at[1], narrow_ref.at[coefs + rank :, half:]),
        (latent_ref, own_ref),
        (out_ref.at[:, pl.ds(pl.multiple_of((1 - lax.axis_index("sub")) * half, LANES), half)], send_ref),
        (into_ref.at[: held_ref.shape[0]], held_ref),
    ]
    copies = [pltpu.make_async_copy(src, dst, sems.at[i]) for i, (src, dst) in enumerate(moves)]
    for copy in copies:
        copy.start()
    for copy in copies[: 2 + len(vectors)]:
        copy.wait()
    wide_ref[:taps] = conv_buf[...]
    for i, buf in enumerate(vector_bufs):
        wide_ref[taps + i : taps + i + 1] = buf[...].reshape(1, buf.shape[0])
    wide_ref[taps + 3 : taps + 4] = jnp.zeros((1, wide_ref.shape[1]), jnp.float32)
    wide_ref[taps + 4 :] = -LOG2_E * jnp.exp(decay_buf[...])
    for copy in copies[2 + len(vectors) :]:
        copy.wait()


def prepare_kernel(lead, order_ref, frequency_ref, mod_ref, narrow_ref, pick_ref, live_ref, rows_ref):
    height = order_ref.shape[0] - 1
    tokens = pick_ref.shape[1]
    width, half = tokens // height, mod_ref.shape[-1]
    own_row = lax.axis_index("rows") * lax.axis_size("cols") + lax.axis_index("cols")
    position = jnp.int32(0)
    for k in range(height):
        position = jnp.where(order_ref[k] == own_row, k, position)
    core = lax.axis_index("sub")
    slot = lax.broadcasted_iota(jnp.int32, (width, 2 * tokens), 0)
    column = lax.broadcasted_iota(jnp.int32, (width, 2 * tokens), 1)
    halves = ([], [])
    for j in range(height):
        block = order_ref[jnp.maximum(position - j, 0)] ^ own_row
        side = core
        for bit in range(height.bit_length() - 1):
            side = side ^ ((block >> bit) & 1)
        for part in range(2):
            start = (block + (side ^ part) * height) * width
            target = jnp.where(position >= j, start, -width) + slot
            halves[part].append(jnp.where(column == target, 1.0, 0.0))
        live_ref[j * width : (j + 1) * width] = jnp.full((width, LANES), jnp.where(position >= j, 1.0, 0.0))
    for part in range(2):
        pick_ref[part] = jnp.concatenate(halves[part], axis=0).astype(jnp.bfloat16)
    moment = jnp.full(frequency_ref.shape, order_ref[height]).astype(jnp.float32)
    angles = jnp.broadcast_to(moment * frequency_ref[...], (16, frequency_ref.shape[1]))
    embed = jnp.concatenate([jnp.cos(angles), jnp.sin(angles)], axis=1).astype(jnp.bfloat16)

    def mod_row(weight):
        return rounded(matmul(embed, weight))[:1]

    for i in range(2):
        mine, other = mod_row(mod_ref[i]), mod_row(narrow_ref[lead:, i * half : (i + 1) * half])
        for part in range(2):
            row = jnp.where(core == part, mine, other)
            rows_ref[2 * i + part : 2 * i + part + 1] = row if i else 1.0 + row
    rows_ref[4:5] = mod_row(mod_ref[2])


def block_kernel(
    taps,
    states,
    rank,
    pick_ref,
    live_ref,
    rows_ref,
    mine_ref,
    other_ref,
    in_mine,
    in_other,
    narrow_mine,
    narrow_other,
    wide_mine,
    wide_other,
    out_mine,
    out_other,
    result_ref,
    act_ref,
    pre_ref,
    weight_ref,
):
    height, width, half = mine_ref.shape
    tokens = height * width
    inner = in_mine.shape[-1]
    core = lax.axis_index("sub")
    coefs = rank + 2 * states
    gate_row = rows_ref[4:5]

    gathered = jnp.concatenate([ref[...].reshape(tokens, half) for ref in (mine_ref, other_ref)], axis=0)
    halves = [matmul(pick_ref[part], gathered) for part in range(2)]
    total = jnp.sum(halves[0] * halves[0] + halves[1] * halves[1], axis=-1, keepdims=True)
    scaling = lax.rsqrt(total / (2.0 * half) + EPSILON)
    live = live_ref[...]
    live_half = jnp.concatenate([live] * (half // LANES), axis=1)
    normed = jnp.concatenate(
        [
            (halves[part] * scaling * rows_ref[part : part + 1] + rows_ref[part + 2 : part + 3]) * live_half
            for part in range(2)
        ],
        axis=1,
    ).astype(jnp.bfloat16)
    own_normed = normed[:width]

    sides = ((in_mine, narrow_mine, wide_mine, out_mine), (in_other, narrow_other, wide_other, out_other))
    selected = None
    for side, (in_ref, narrow, wide, _) in enumerate(sides):
        seq = rounded(matmul(normed, in_ref[0]))
        pieces = []
        for j in range(height):
            mixed = wide[taps : taps + 1, :]
            for back in range(min(taps, height - j)):
                tap = taps - 1 - back
                mixed = mixed + wide[tap : tap + 1, :] * seq[(j + back) * width : (j + back + 1) * width]
            pieces.append(silu(mixed))
        act = jnp.concatenate(pieces, axis=0).astype(jnp.bfloat16)
        act_ref[side] = act.astype(jnp.float32)
        part = lax.dot_general(
            act, narrow[:coefs, :], (((1,), (1,)), ((), ())), preferred_element_type=jnp.float32
        )
        selected = part if selected is None else selected + part

    low_rank = selected[:, :rank].astype(jnp.bfloat16)
    for side, (_, narrow, _, _) in enumerate(sides):
        pre_ref[side] = matmul(low_rank, narrow[coefs : coefs + rank, :])
    own_exit = selected[:width, rank + states :]
    for j in range(height):
        product = selected[j * width : (j + 1) * width, rank : rank + states] * own_exit
        for n in range(states):
            weight_ref[j, n] = jnp.broadcast_to(product[:, n : n + 1], (width, LANES))

    update = None
    columns = pl.ds(pl.multiple_of(core * half, LANES), half)
    for side, (in_ref, _, wide, out_ref) in enumerate(sides):
        gate = silu(rounded(matmul(own_normed, in_ref[1])))
        rates = wide[taps + 4 :, :]
        step_bias, skip = wide[taps + 1 : taps + 2, :], wide[taps + 2 : taps + 3, :]
        outs = []
        for block in range(inner // LANES):
            lanes = slice(block * LANES, (block + 1) * LANES)
            size = softplus(pre_ref[side, :, lanes] + step_bias[:, lanes])
            act = act_ref[side, :, lanes]
            drive = size * act * live
            rate = [jnp.broadcast_to(rates[n : n + 1, lanes], (width, LANES)) for n in range(states)]
            scanned = skip[:, lanes] * act[:width]
            elapsed = None
            for j in range(height):
                rows = slice(j * width, (j + 1) * width)
                mixed = None
                for n in range(states):
                    term = weight_ref[j, n]
                    if j:
                        term = jnp.exp2(elapsed * rate[n]) * term
                    mixed = term if mixed is None else mixed + term
                scanned = scanned + drive[rows] * mixed
                elapsed = size[rows] if elapsed is None else elapsed + size[rows]
            outs.append((scanned * gate[:, lanes]).astype(jnp.bfloat16))
        part = matmul(jnp.concatenate(outs, axis=1), out_ref[...] if side else out_ref[:, columns])
        update = part if update is None else update + part
    own_latent = mine_ref[0].astype(jnp.float32)
    result_ref[...] = (own_latent + gate_row * rounded(update)).astype(jnp.bfloat16)


def gather_device(
    latents,
    timestep,
    scan_order,
    modulation,
    input_proj,
    conv_weight,
    conv_bias,
    select_proj,
    step_proj,
    step_bias,
    decay_log,
    skip_gain,
    output_proj,
):
    _, width, half = latents.shape
    lines = lax.axis_size(("rows", "cols"))
    inner, states = input_proj.shape[-1], decay_log.shape[0]
    taps, rank = conv_weight.shape[0], step_proj.shape[0]
    tokens = lines * width
    freq_count = modulation.shape[0]
    vmem = pl.BlockSpec(memory_space=pltpu.VMEM)
    smem = pl.BlockSpec(memory_space=pltpu.SMEM)
    by_row = modulation.transpose(1, 0, 2)
    coefs = select_proj.shape[1]
    cut = input_proj.shape[0] // 3 if input_proj.shape[0] % 3 == 0 else input_proj.shape[0] // 2
    halfway = freq_count // 2
    frequency = jnp.exp(-math.log(10000.0) * jnp.arange(halfway, dtype=jnp.float32) / halfway)[None]
    anywhere = pl.BlockSpec(memory_space=pl.ANY)
    narrow, wide, held, own, out_send = pl.pallas_call(
        fetch_kernel,
        out_shape=(
            jax.ShapeDtypeStruct((coefs + rank + freq_count, inner), jnp.bfloat16),
            jax.ShapeDtypeStruct((taps + 4 + states, inner), jnp.float32),
            jax.ShapeDtypeStruct((cut,) + input_proj.shape[1:], jnp.bfloat16),
            jax.ShapeDtypeStruct(latents.shape, jnp.bfloat16),
            jax.ShapeDtypeStruct((inner, half), jnp.bfloat16),
        ),
        in_specs=[anywhere] * 11,
        out_specs=[vmem] * 5,
        scratch_shapes=[
            pltpu.VMEM(conv_weight.shape, jnp.float32),
            pltpu.VMEM(decay_log.shape, jnp.float32),
            [pltpu.VMEM(conv_bias.shape, jnp.float32)] * 3,
            pltpu.SemaphoreType.DMA((12,)),
        ],
        compiler_params=pltpu.CompilerParams(vmem_limit_bytes=8 << 20),
        name="fetch",
    )(
        *(
            pltpu.with_memory_space_constraint(tensor, pltpu.HBM)
            for tensor in (
                select_proj.T,
                step_proj,
                by_row,
                input_proj,
                conv_weight,
                decay_log,
                conv_bias,
                step_bias,
                skip_gain,
                latents,
                output_proj,
            )
        )
    )
    gathered = latents
    reach, hop = 1, 0
    out_other = swap_cores(out_send)
    while reach < lines:
        pairs = [(i, i ^ (2 * reach + 1)) for i in range(2 * lines)]
        arrived = lax.ppermute(gathered, ("rows", "cols", "sub"), pairs)
        gathered = jnp.concatenate([gathered if hop else own, arrived], 0)
        reach, hop = 2 * reach, hop + 1
    other = swap_cores(gathered)
    rest = input_proj[cut:].transpose(1, 0, 2)
    into = jnp.concatenate([held.transpose(1, 0, 2), rest], axis=1)
    into_other = swap_cores(into)
    narrow_other = swap_cores(narrow)
    wide_other = swap_cores(wide)
    scalars = jnp.concatenate([scan_order, timestep])
    pick, live, rows = pl.pallas_call(
        functools.partial(prepare_kernel, coefs + rank),
        out_shape=(
            jax.ShapeDtypeStruct((2, tokens, 2 * tokens), jnp.bfloat16),
            jax.ShapeDtypeStruct((tokens, LANES), jnp.float32),
            jax.ShapeDtypeStruct((8, half), jnp.float32),
        ),
        in_specs=[smem, vmem, vmem, vmem],
        out_specs=(vmem, vmem, vmem),
        compiler_params=pltpu.CompilerParams(vmem_limit_bytes=8 << 20),
        name="prepare",
    )(scalars, frequency, by_row, narrow_other)
    operands = (
        pick,
        live,
        rows,
        gathered,
        other,
        into,
        into_other,
        narrow,
        narrow_other,
        wide,
        wide_other,
        output_proj,
        out_other,
    )
    result = pl.pallas_call(
        functools.partial(block_kernel, taps, states, rank),
        out_shape=jax.ShapeDtypeStruct((width, half), jnp.bfloat16),
        in_specs=[vmem] * len(operands),
        out_specs=vmem,
        scratch_shapes=[
            pltpu.VMEM((2, tokens, inner), jnp.float32),
            pltpu.VMEM((2, tokens, inner), jnp.float32),
            pltpu.VMEM((lines, states, width, LANES), jnp.float32),
        ],
        compiler_params=pltpu.CompilerParams(vmem_limit_bytes=16 << 20),
        name="scan_block",
    )(*operands)
    return result[None]


def on_device(latents, *others):
    rows_dev, grid_width, half = latents.shape
    lines = lax.axis_size(("rows", "cols"))
    small = rows_dev == 1 and lines & (lines - 1) == 0 and lines * grid_width <= TOKEN_LIMIT
    tiled = grid_width % 8 == 0 and half % LANES == 0 and lax.axis_size("sub") == 2
    run = gather_device if small and tiled else exchange_device
    return run(latents, *others)


def solution(mesh):
    placed = (
        P(("groups", "rows", "cols"), None, "sub"),
        P("groups"),
        P(),
        P(None, None, "sub"),
        P(None, None, "sub"),
        P(None, "sub"),
        P("sub"),
        P("sub", None),
        P(None, "sub"),
        P("sub"),
        P(None, "sub"),
        P("sub"),
        P("sub", None),
    )
    return jax.shard_map(
        on_device,
        mesh=mesh,
        in_specs=placed,
        out_specs=P(("groups", "rows", "cols"), None, "sub"),
        check_vma=False,
    )
```

```python
import functools
import math

import jax
import jax.numpy as jnp
from jax import lax
from jax.experimental import pallas as pl
from jax.experimental.pallas import tpu as pltpu
from jax.sharding import PartitionSpec as P


NS = 16
RANK = 48


EPSILON = 1e-06


def embed_time(timestep, freq_count):
    halfway = freq_count // 2
    frequency = jnp.exp(-math.log(10000.0) * jnp.arange(halfway, dtype=jnp.float32) / halfway)
    angles = timestep.astype(jnp.float32)[0] * frequency
    return jnp.concatenate([jnp.cos(angles), jnp.sin(angles)]).astype(jnp.bfloat16)


def widen(latent_half, scale_shift):
    return (
        lax.all_gather(latent_half, "sub", axis=2, tiled=True),
        lax.all_gather(scale_shift, "sub", axis=1, tiled=True),
    )


def normalize(latent_full, scale_full):
    values = latent_full.astype(jnp.float32)
    meansq = jnp.mean(values * values, axis=-1, keepdims=True)
    scaled = values * lax.rsqrt(meansq + EPSILON)
    scale_row = scale_full[0].astype(jnp.float32)
    shift_row = scale_full[1].astype(jnp.float32)
    return (scaled * (1.0 + scale_row) + shift_row).astype(jnp.bfloat16)


def project_in(normed, input_proj):
    model_width = input_proj.shape[0]
    flat_weight = input_proj.reshape(model_width, -1)
    result = jnp.dot(
        normed.reshape(-1, model_width), flat_weight, preferred_element_type=jnp.float32
    )
    return result.astype(jnp.bfloat16).reshape(normed.shape[:-1] + (flat_weight.shape[1],))


def reorder(one_hot, sequence):
    return jnp.einsum("kh,hnc->knc", one_hot, sequence, preferred_element_type=jnp.float32).astype(
        jnp.bfloat16
    )


def restore(one_hot, sequence):
    return jnp.einsum("kh,knc->hnc", one_hot, sequence, preferred_element_type=jnp.float32).astype(
        jnp.bfloat16
    )


def scan_columns(
    projected, conv_weight, conv_bias, select_proj, step_proj, step_bias, decay_log, skip_gain
):
    height, item_count, doubled = projected.shape
    inner_width = doubled // 2
    seq_input = projected[..., :inner_width].astype(jnp.float32)
    seq_gate = projected[..., inner_width:].astype(jnp.float32)
    tap_count = conv_weight.shape[0]
    padded = jnp.pad(seq_input, ((tap_count - 1, 0), (0, 0), (0, 0)))
    conv_sum = conv_bias + jnp.zeros_like(seq_input)
    for offset in range(tap_count):
        conv_sum = conv_sum + conv_weight[offset] * padded[offset : offset + height]
    activated = jax.nn.silu(conv_sum).astype(jnp.bfloat16)
    flat_act = activated.reshape(height * item_count, inner_width)
    partial_value = lax.dot_general(
        select_proj, flat_act, (((0,), (1,)), ((), ())), preferred_element_type=jnp.float32
    )
    selected = lax.psum(partial_value, "sub")
    step_low = selected[:RANK].astype(jnp.bfloat16)
    step_pre = lax.dot_general(
        step_low, step_proj, (((0,), (0,)), ((), ())), preferred_element_type=jnp.float32
    )
    step_size = jax.nn.softplus(step_pre + step_bias).reshape(height, item_count, inner_width)
    entry_coef = selected[RANK : RANK + NS].T.reshape(height, item_count, NS)
    exit_coef = selected[RANK + NS :].T.reshape(height, item_count, NS)
    act_float = activated.astype(jnp.float32)
    decay_rate = -jnp.exp(decay_log)
    block_len = height // 16 if height % 16 == 0 else height
    blocks = height // block_len

    def split_blocks(tensor):
        return tensor.reshape((blocks, block_len) + tensor.shape[1:])

    def combine(earlier, latter):
        return (earlier[0] * latter[0], latter[0] * earlier[1] + latter[1])

    def advance(carried, pieces):
        step_blk, act_blk, entry_blk, exit_blk = pieces
        decays = jnp.exp(step_blk[:, :, None, :] * decay_rate)
        driving = (step_blk * act_blk)[:, :, None, :] * entry_blk[..., None]
        cum_decay, cum_drive = lax.associative_scan(combine, (decays, driving), axis=0)
        states = cum_drive + cum_decay * carried[None]
        output = jnp.sum(exit_blk[..., None] * states, axis=2) + skip_gain * act_blk
        return (states[-1], output)

    initial = jnp.zeros((item_count, NS, inner_width), jnp.float32)
    pieces_all = (
        split_blocks(step_size),
        split_blocks(act_float),
        split_blocks(entry_coef),
        split_blocks(exit_coef),
    )
    _, outputs = lax.scan(advance, initial, pieces_all)
    scanned = outputs.reshape(height, item_count, inner_width)
    return (scanned * jax.nn.silu(seq_gate)).astype(jnp.bfloat16)


def exchange_device(
    latents,
    timestep,
    scan_order,
    modulation,
    input_proj,
    conv_weight,
    conv_bias,
    select_proj,
    step_proj,
    step_bias,
    decay_log,
    skip_gain,
    output_proj,
):
    rows_dev, grid_width, half_model = latents.shape
    line_groups = lax.axis_size(("rows", "cols"))
    cols_dev = grid_width // line_groups
    height = rows_dev * line_groups
    inner_width = input_proj.shape[2]
    freq_count = modulation.shape[0]
    time_embed = embed_time(timestep, freq_count)
    mod_rows = jnp.dot(
        time_embed[None, :], modulation.reshape(freq_count, -1), preferred_element_type=jnp.float32
    )
    mod_rows = mod_rows.reshape(3, half_model).astype(jnp.bfloat16)
    scale_shift = mod_rows[:2]
    gate_row = mod_rows[2].astype(jnp.float32)
    one_hot = (scan_order[:, None] == jnp.arange(height, dtype=jnp.int32)[None, :]).astype(
        jnp.bfloat16
    )
    latent_full, scale_full = widen(latents, scale_shift)
    projected = project_in(normalize(latent_full, scale_full), input_proj)
    sectioned = projected.reshape(rows_dev, line_groups, cols_dev, 2 * inner_width)[None]
    received = lax.all_to_all(sectioned, ("rows", "cols"), split_axis=2, concat_axis=0, tiled=True)
    item_count = received.shape[3]
    ordered = reorder(one_hot, received.reshape(height, item_count, 2 * inner_width))
    gated = scan_columns(
        ordered, conv_weight, conv_bias, select_proj, step_proj, step_bias, decay_log, skip_gain
    )
    placed = restore(one_hot, gated)
    returned = lax.all_to_all(
        placed.reshape(line_groups, rows_dev, 1, item_count, inner_width),
        ("rows", "cols"),
        split_axis=0,
        concat_axis=2,
        tiled=True,
    )
    gathered = returned.reshape(rows_dev, line_groups, item_count, inner_width)
    partial_value = jnp.dot(
        gathered.reshape(rows_dev * grid_width, inner_width),
        output_proj,
        preferred_element_type=jnp.float32,
    )
    summed = lax.psum_scatter(
        partial_value.reshape(rows_dev, grid_width, -1).astype(jnp.bfloat16),
        "sub",
        scatter_dimension=2,
        tiled=True,
    )
    blended = latents.astype(jnp.float32) + gate_row * summed.astype(jnp.float32)
    return blended.astype(jnp.bfloat16)


LANES = 128
TOKEN_LIMIT = 256
STRIDE = 2
LOG2_E = math.log2(math.e)


def hops(lines):
    count = lines.bit_length() - 1
    return [1 << i for i in sorted(range(count), key=lambda i: (i != count - 1, i))]


def swap_cores(tensor):
    return lax.ppermute(tensor, "sub", [(0, 1), (1, 0)])


def silu(values):
    half = 0.5 * values
    return half + half * jnp.tanh(half)


def softplus(values):
    return jnp.maximum(values, 0.0) + jnp.log(1.0 + jnp.exp(-jnp.abs(values)))


def matmul(left, right):
    return jnp.dot(left, right, preferred_element_type=jnp.float32)


def rounded(values):
    return values.astype(jnp.bfloat16).astype(jnp.float32)


def fetch_kernel(
    sel_ref,
    step_ref,
    mod_ref,
    into_ref,
    conv_ref,
    decay_ref,
    bias_ref,
    stepb_ref,
    skip_ref,
    latent_ref,
    out_ref,
    narrow_ref,
    wide_ref,
    held_ref,
    own_ref,
    send_ref,
    conv_buf,
    decay_buf,
    vector_bufs,
    sems,
):
    coefs, rank, taps = sel_ref.shape[0], step_ref.shape[0], conv_ref.shape[0]
    half = mod_ref.shape[-1]
    vectors = (bias_ref, stepb_ref, skip_ref)
    moves = [
        (conv_ref, conv_buf),
        (decay_ref, decay_buf),
        *((ref, vector_bufs[i]) for i, ref in enumerate(vectors)),
        (sel_ref, narrow_ref.at[:coefs]),
        (step_ref, narrow_ref.at[coefs : coefs + rank]),
        (mod_ref.at[0], narrow_ref.at[coefs + rank :, :half]),
        (mod_ref.at[1], narrow_ref.at[coefs + rank :, half:]),
        (latent_ref, own_ref),
        (out_ref.at[:, pl.ds(pl.multiple_of((1 - lax.axis_index("sub")) * half, LANES), half)], send_ref),
        (into_ref.at[: held_ref.shape[0]], held_ref),
    ]
    copies = [pltpu.make_async_copy(src, dst, sems.at[i]) for i, (src, dst) in enumerate(moves)]
    for copy in copies:
        copy.start()
    for copy in copies[: 2 + len(vectors)]:
        copy.wait()
    wide_ref[:taps] = conv_buf[...]
    for i, buf in enumerate(vector_bufs):
        wide_ref[taps + i : taps + i + 1] = buf[...].reshape(1, buf.shape[0])
    wide_ref[taps + 3 : taps + 4] = jnp.zeros((1, wide_ref.shape[1]), jnp.float32)
    wide_ref[taps + 4 :] = -LOG2_E * jnp.exp(decay_buf[...])
    for copy in copies[2 + len(vectors) :]:
        copy.wait()


def prepare_kernel(lead, order_ref, frequency_ref, mod_ref, narrow_ref, pick_ref, live_ref, rows_ref):
    height = order_ref.shape[0] - 1
    tokens = pick_ref.shape[1]
    width, half = tokens // height, mod_ref.shape[-1]
    own_row = lax.axis_index("rows") * lax.axis_size("cols") + lax.axis_index("cols")
    position = jnp.int32(0)
    for k in range(height):
        position = jnp.where(order_ref[k] == own_row, k, position)
    core = lax.axis_index("sub")
    slot = lax.broadcasted_iota(jnp.int32, (width, 2 * tokens), 0)
    column = lax.broadcasted_iota(jnp.int32, (width, 2 * tokens), 1)
    halves = ([], [])
    for j in range(height):
        away = order_ref[jnp.maximum(position - j, 0)] ^ own_row
        side, block = core, jnp.int32(0)
        for hop, reach in enumerate(hops(height)):
            crossed = (away // reach) & 1
            side, block = side ^ crossed, block + (crossed << hop)
        for part in range(2):
            start = (block + (side ^ part) * height) * width
            target = jnp.where(position >= j, start, -width) + slot
            halves[part].append(jnp.where(column == target, 1.0, 0.0))
        live_ref[j * width : (j + 1) * width] = jnp.full((width, LANES), jnp.where(position >= j, 1.0, 0.0))
    for part in range(2):
        pick_ref[part] = jnp.concatenate(halves[part], axis=0).astype(jnp.bfloat16)
    moment = jnp.full(frequency_ref.shape, order_ref[height]).astype(jnp.float32)
    angles = jnp.broadcast_to(moment * frequency_ref[...], (16, frequency_ref.shape[1]))
    embed = jnp.concatenate([jnp.cos(angles), jnp.sin(angles)], axis=1).astype(jnp.bfloat16)

    def mod_row(weight):
        return rounded(matmul(embed, weight))[:1]

    for i in range(2):
        mine, other = mod_row(mod_ref[i]), mod_row(narrow_ref[lead:, i * half : (i + 1) * half])
        for part in range(2):
            row = jnp.where(core == part, mine, other)
            rows_ref[2 * i + part : 2 * i + part + 1] = row if i else 1.0 + row
    rows_ref[4:5] = mod_row(mod_ref[2])


def block_kernel(
    taps,
    states,
    rank,
    pick_ref,
    live_ref,
    rows_ref,
    mine_ref,
    other_ref,
    in_mine,
    in_other,
    narrow_mine,
    narrow_other,
    wide_mine,
    wide_other,
    out_mine,
    out_other,
    result_ref,
    act_ref,
    pre_ref,
    weight_ref,
    gate_ref,
    product_ref,
    latest_ref,
):
    height, width, half = mine_ref.shape
    tokens = height * width
    inner = in_mine.shape[-1]
    core = lax.axis_index("sub")
    coefs = rank + 2 * states
    gate_row = rows_ref[4:5]

    gathered = jnp.concatenate([ref[...].reshape(tokens, half) for ref in (mine_ref, other_ref)], axis=0)
    halves = [matmul(pick_ref[part], gathered) for part in range(2)]
    total = jnp.sum(halves[0] * halves[0] + halves[1] * halves[1], axis=-1, keepdims=True)
    scaling = lax.rsqrt(total / (2.0 * half) + EPSILON)
    live = live_ref[...]
    visited = jnp.sum(live[:, :1]) / width
    live_half = jnp.concatenate([live] * (half // LANES), axis=1)
    normed = jnp.concatenate(
        [
            (halves[part] * scaling * rows_ref[part : part + 1] + rows_ref[part + 2 : part + 3]) * live_half
            for part in range(2)
        ],
        axis=1,
    ).astype(jnp.bfloat16)
    own_normed = normed[:width]

    sides = ((in_mine, narrow_mine, wide_mine, out_mine), (in_other, narrow_other, wide_other, out_other))
    selected = None
    sequences = [rounded(matmul(normed, in_ref[0])) for in_ref, _, _, _ in sides]
    for side, (in_ref, _, _, _) in enumerate(sides):
        gate_ref[side] = silu(rounded(matmul(own_normed, in_ref[1])))
    for side, (_, narrow, wide, _) in enumerate(sides):
        seq = sequences[side]
        pieces = []
        for j in range(height):
            mixed = wide[taps : taps + 1, :]
            for back in range(min(taps, height - j)):
                tap = taps - 1 - back
                mixed = mixed + wide[tap : tap + 1, :] * seq[(j + back) * width : (j + back + 1) * width]
            pieces.append(silu(mixed))
        act = jnp.concatenate(pieces, axis=0).astype(jnp.bfloat16)
        act_ref[side] = act.astype(jnp.float32)
        part = lax.dot_general(
            act, narrow[:coefs, :], (((1,), (1,)), ((), ())), preferred_element_type=jnp.float32
        )
        selected = part if selected is None else selected + part

    low_rank = selected[:, :rank].astype(jnp.bfloat16)
    for side, (_, narrow, _, _) in enumerate(sides):
        pre_ref[side] = matmul(low_rank, narrow[coefs : coefs + rank, :])
    own_exit = selected[:width, rank + states :]
    own_product = selected[:width, rank : rank + states] * own_exit
    latest_ref[...] = jnp.broadcast_to(jnp.sum(own_product, axis=1, keepdims=True), (width, LANES))
    for j in range(1, height):
        rows = slice(j * width, (j + 1) * width)
        product_ref[rows] = selected[rows, rank : rank + states] * own_exit * live[rows, :states]

    def finish(count):
        for j in range(1, count):
            product = product_ref[j * width : (j + 1) * width]
            for n in range(states):
                weight_ref[j, n] = jnp.broadcast_to(product[:, n : n + 1], (width, LANES))
        latest = latest_ref[...]
        update = None
        columns = pl.ds(pl.multiple_of(core * half, LANES), half)
        for side, (_, _, wide, out_ref) in enumerate(sides):
            rates = wide[taps + 4 :, :]
            step_bias, skip = wide[taps + 1 : taps + 2, :], wide[taps + 2 : taps + 3, :]
            outs = []
            for block in range(inner // LANES):
                lanes = slice(block * LANES, (block + 1) * LANES)
                size = softplus(pre_ref[side, : count * width, lanes] + step_bias[:, lanes])
                act = act_ref[side, : count * width, lanes]
                drive = size * act
                rate = [jnp.broadcast_to(rates[n : n + 1, lanes], (width, LANES)) for n in range(states)]
                scanned = skip[:, lanes] * act[:width] + drive[:width] * latest
                elapsed = size[:width]
                for j in range(1, count):
                    rows = slice(j * width, (j + 1) * width)
                    mixed = None
                    for n in range(states):
                        term = jnp.exp2(elapsed * rate[n]) * weight_ref[j, n]
                        mixed = term if mixed is None else mixed + term
                    scanned = scanned + drive[rows] * mixed
                    elapsed = elapsed + size[rows]
                outs.append((scanned * gate_ref[side, :, lanes]).astype(jnp.bfloat16))
            part = matmul(jnp.concatenate(outs, axis=1), out_ref[...] if side else out_ref[:, columns])
            update = part if update is None else update + part
        own_latent = mine_ref[0].astype(jnp.float32)
        result_ref[...] = (own_latent + gate_row * rounded(update)).astype(jnp.bfloat16)

    for start in range(0, height, STRIDE):
        last = start + STRIDE >= height
        chosen = visited > start if last else (visited > start) & (visited <= start + STRIDE)
        pl.when(chosen)(functools.partial(finish, height if last else start + STRIDE))


def gather_device(
    latents,
    timestep,
    scan_order,
    modulation,
    input_proj,
    conv_weight,
    conv_bias,
    select_proj,
    step_proj,
    step_bias,
    decay_log,
    skip_gain,
    output_proj,
):
    _, width, half = latents.shape
    lines = lax.axis_size(("rows", "cols"))
    inner, states = input_proj.shape[-1], decay_log.shape[0]
    taps, rank = conv_weight.shape[0], step_proj.shape[0]
    tokens = lines * width
    freq_count = modulation.shape[0]
    vmem = pl.BlockSpec(memory_space=pltpu.VMEM)
    smem = pl.BlockSpec(memory_space=pltpu.SMEM)
    by_row = modulation.transpose(1, 0, 2)
    coefs = select_proj.shape[1]
    cut = input_proj.shape[0] // 3 if input_proj.shape[0] % 3 == 0 else input_proj.shape[0] // 2
    halfway = freq_count // 2
    frequency = jnp.exp(-math.log(10000.0) * jnp.arange(halfway, dtype=jnp.float32) / halfway)[None]
    anywhere = pl.BlockSpec(memory_space=pl.ANY)
    narrow, wide, held, own, out_send = pl.pallas_call(
        fetch_kernel,
        out_shape=(
            jax.ShapeDtypeStruct((coefs + rank + freq_count, inner), jnp.bfloat16),
            jax.ShapeDtypeStruct((taps + 4 + states, inner), jnp.float32),
            jax.ShapeDtypeStruct((cut,) + input_proj.shape[1:], jnp.bfloat16),
            jax.ShapeDtypeStruct(latents.shape, jnp.bfloat16),
            jax.ShapeDtypeStruct((inner, half), jnp.bfloat16),
        ),
        in_specs=[anywhere] * 11,
        out_specs=[vmem] * 5,
        scratch_shapes=[
            pltpu.VMEM(conv_weight.shape, jnp.float32),
            pltpu.VMEM(decay_log.shape, jnp.float32),
            [pltpu.VMEM(conv_bias.shape, jnp.float32)] * 3,
            pltpu.SemaphoreType.DMA((12,)),
        ],
        compiler_params=pltpu.CompilerParams(vmem_limit_bytes=8 << 20),
        name="fetch",
    )(
        *(
            pltpu.with_memory_space_constraint(tensor, pltpu.HBM)
            for tensor in (
                select_proj.T,
                step_proj,
                by_row,
                input_proj,
                conv_weight,
                decay_log,
                conv_bias,
                step_bias,
                skip_gain,
                latents,
                output_proj,
            )
        )
    )
    gathered = latents
    out_other = swap_cores(out_send)
    for hop, reach in enumerate(hops(lines)):
        pairs = [(i, i ^ (2 * reach + 1)) for i in range(2 * lines)]
        arrived = lax.ppermute(gathered, ("rows", "cols", "sub"), pairs)
        gathered = jnp.concatenate([gathered if hop else own, arrived], 0)
    other = swap_cores(gathered)
    rest = input_proj[cut:].transpose(1, 0, 2)
    into = jnp.concatenate([held.transpose(1, 0, 2), rest], axis=1)
    into_other = swap_cores(into)
    narrow_other = swap_cores(narrow)
    wide_other = swap_cores(wide)
    scalars = jnp.concatenate([scan_order, timestep])
    pick, live, rows = pl.pallas_call(
        functools.partial(prepare_kernel, coefs + rank),
        out_shape=(
            jax.ShapeDtypeStruct((2, tokens, 2 * tokens), jnp.bfloat16),
            jax.ShapeDtypeStruct((tokens, LANES), jnp.float32),
            jax.ShapeDtypeStruct((8, half), jnp.float32),
        ),
        in_specs=[smem, vmem, vmem, vmem],
        out_specs=(vmem, vmem, vmem),
        compiler_params=pltpu.CompilerParams(vmem_limit_bytes=8 << 20),
        name="prepare",
    )(scalars, frequency, by_row, narrow_other)
    operands = (
        pick,
        live,
        rows,
        gathered,
        other,
        into,
        into_other,
        narrow,
        narrow_other,
        wide,
        wide_other,
        output_proj,
        out_other,
    )
    result = pl.pallas_call(
        functools.partial(block_kernel, taps, states, rank),
        out_shape=jax.ShapeDtypeStruct((width, half), jnp.bfloat16),
        in_specs=[vmem] * len(operands),
        out_specs=vmem,
        scratch_shapes=[
            pltpu.VMEM((2, tokens, inner), jnp.float32),
            pltpu.VMEM((2, tokens, inner), jnp.float32),
            pltpu.VMEM((lines, states, width, LANES), jnp.float32),
            pltpu.VMEM((2, width, inner), jnp.float32),
            pltpu.VMEM((tokens, states), jnp.float32),
            pltpu.VMEM((width, LANES), jnp.float32),
        ],
        compiler_params=pltpu.CompilerParams(vmem_limit_bytes=16 << 20),
        name="scan_block",
    )(*operands)
    return result[None]


def on_device(latents, *others):
    rows_dev, grid_width, half = latents.shape
    lines = lax.axis_size(("rows", "cols"))
    small = rows_dev == 1 and lines & (lines - 1) == 0 and lines * grid_width <= TOKEN_LIMIT
    tiled = grid_width % 8 == 0 and half % LANES == 0 and lax.axis_size("sub") == 2
    run = gather_device if small and tiled else exchange_device
    return run(latents, *others)


def solution(mesh):
    placed = (
        P(("groups", "rows", "cols"), None, "sub"),
        P("groups"),
        P(),
        P(None, None, "sub"),
        P(None, None, "sub"),
        P(None, "sub"),
        P("sub"),
        P("sub", None),
        P(None, "sub"),
        P("sub"),
        P(None, "sub"),
        P("sub"),
        P("sub", None),
    )
    return jax.shard_map(
        on_device,
        mesh=mesh,
        in_specs=placed,
        out_specs=P(("groups", "rows", "cols"), None, "sub"),
        check_vma=False,
    )
```

```python
import functools
import math

import jax
import jax.numpy as jnp
from jax import lax
from jax.experimental import pallas as pl
from jax.experimental.pallas import tpu as pltpu
from jax.sharding import PartitionSpec as P


NS = 16
RANK = 48


EPSILON = 1e-06


def embed_time(timestep, freq_count):
    halfway = freq_count // 2
    frequency = jnp.exp(-math.log(10000.0) * jnp.arange(halfway, dtype=jnp.float32) / halfway)
    angles = timestep.astype(jnp.float32)[0] * frequency
    return jnp.concatenate([jnp.cos(angles), jnp.sin(angles)]).astype(jnp.bfloat16)


def widen(latent_half, scale_shift):
    return (
        lax.all_gather(latent_half, "sub", axis=2, tiled=True),
        lax.all_gather(scale_shift, "sub", axis=1, tiled=True),
    )


def normalize(latent_full, scale_full):
    values = latent_full.astype(jnp.float32)
    meansq = jnp.mean(values * values, axis=-1, keepdims=True)
    scaled = values * lax.rsqrt(meansq + EPSILON)
    scale_row = scale_full[0].astype(jnp.float32)
    shift_row = scale_full[1].astype(jnp.float32)
    return (scaled * (1.0 + scale_row) + shift_row).astype(jnp.bfloat16)


def project_in(normed, input_proj):
    model_width = input_proj.shape[0]
    flat_weight = input_proj.reshape(model_width, -1)
    result = jnp.dot(
        normed.reshape(-1, model_width), flat_weight, preferred_element_type=jnp.float32
    )
    return result.astype(jnp.bfloat16).reshape(normed.shape[:-1] + (flat_weight.shape[1],))


def reorder(one_hot, sequence):
    return jnp.einsum("kh,hnc->knc", one_hot, sequence, preferred_element_type=jnp.float32).astype(
        jnp.bfloat16
    )


def restore(one_hot, sequence):
    return jnp.einsum("kh,knc->hnc", one_hot, sequence, preferred_element_type=jnp.float32).astype(
        jnp.bfloat16
    )


def scan_columns(
    projected, conv_weight, conv_bias, select_proj, step_proj, step_bias, decay_log, skip_gain
):
    height, item_count, doubled = projected.shape
    inner_width = doubled // 2
    seq_input = projected[..., :inner_width].astype(jnp.float32)
    seq_gate = projected[..., inner_width:].astype(jnp.float32)
    tap_count = conv_weight.shape[0]
    padded = jnp.pad(seq_input, ((tap_count - 1, 0), (0, 0), (0, 0)))
    conv_sum = conv_bias + jnp.zeros_like(seq_input)
    for offset in range(tap_count):
        conv_sum = conv_sum + conv_weight[offset] * padded[offset : offset + height]
    activated = jax.nn.silu(conv_sum).astype(jnp.bfloat16)
    flat_act = activated.reshape(height * item_count, inner_width)
    partial_value = lax.dot_general(
        select_proj, flat_act, (((0,), (1,)), ((), ())), preferred_element_type=jnp.float32
    )
    selected = lax.psum(partial_value, "sub")
    step_low = selected[:RANK].astype(jnp.bfloat16)
    step_pre = lax.dot_general(
        step_low, step_proj, (((0,), (0,)), ((), ())), preferred_element_type=jnp.float32
    )
    step_size = jax.nn.softplus(step_pre + step_bias).reshape(height, item_count, inner_width)
    entry_coef = selected[RANK : RANK + NS].T.reshape(height, item_count, NS)
    exit_coef = selected[RANK + NS :].T.reshape(height, item_count, NS)
    act_float = activated.astype(jnp.float32)
    decay_rate = -jnp.exp(decay_log)
    block_len = height // 16 if height % 16 == 0 else height
    blocks = height // block_len

    def split_blocks(tensor):
        return tensor.reshape((blocks, block_len) + tensor.shape[1:])

    def combine(earlier, latter):
        return (earlier[0] * latter[0], latter[0] * earlier[1] + latter[1])

    def advance(carried, pieces):
        step_blk, act_blk, entry_blk, exit_blk = pieces
        decays = jnp.exp(step_blk[:, :, None, :] * decay_rate)
        driving = (step_blk * act_blk)[:, :, None, :] * entry_blk[..., None]
        cum_decay, cum_drive = lax.associative_scan(combine, (decays, driving), axis=0)
        states = cum_drive + cum_decay * carried[None]
        output = jnp.sum(exit_blk[..., None] * states, axis=2) + skip_gain * act_blk
        return (states[-1], output)

    initial = jnp.zeros((item_count, NS, inner_width), jnp.float32)
    pieces_all = (
        split_blocks(step_size),
        split_blocks(act_float),
        split_blocks(entry_coef),
        split_blocks(exit_coef),
    )
    _, outputs = lax.scan(advance, initial, pieces_all)
    scanned = outputs.reshape(height, item_count, inner_width)
    return (scanned * jax.nn.silu(seq_gate)).astype(jnp.bfloat16)


def exchange_device(
    latents,
    timestep,
    scan_order,
    modulation,
    input_proj,
    conv_weight,
    conv_bias,
    select_proj,
    step_proj,
    step_bias,
    decay_log,
    skip_gain,
    output_proj,
):
    rows_dev, grid_width, half_model = latents.shape
    line_groups = lax.axis_size(("rows", "cols"))
    cols_dev = grid_width // line_groups
    height = rows_dev * line_groups
    inner_width = input_proj.shape[2]
    freq_count = modulation.shape[0]
    time_embed = embed_time(timestep, freq_count)
    mod_rows = jnp.dot(
        time_embed[None, :], modulation.reshape(freq_count, -1), preferred_element_type=jnp.float32
    )
    mod_rows = mod_rows.reshape(3, half_model).astype(jnp.bfloat16)
    scale_shift = mod_rows[:2]
    gate_row = mod_rows[2].astype(jnp.float32)
    one_hot = (scan_order[:, None] == jnp.arange(height, dtype=jnp.int32)[None, :]).astype(
        jnp.bfloat16
    )
    latent_full, scale_full = widen(latents, scale_shift)
    projected = project_in(normalize(latent_full, scale_full), input_proj)
    sectioned = projected.reshape(rows_dev, line_groups, cols_dev, 2 * inner_width)[None]
    received = lax.all_to_all(sectioned, ("rows", "cols"), split_axis=2, concat_axis=0, tiled=True)
    item_count = received.shape[3]
    ordered = reorder(one_hot, received.reshape(height, item_count, 2 * inner_width))
    gated = scan_columns(
        ordered, conv_weight, conv_bias, select_proj, step_proj, step_bias, decay_log, skip_gain
    )
    placed = restore(one_hot, gated)
    returned = lax.all_to_all(
        placed.reshape(line_groups, rows_dev, 1, item_count, inner_width),
        ("rows", "cols"),
        split_axis=0,
        concat_axis=2,
        tiled=True,
    )
    gathered = returned.reshape(rows_dev, line_groups, item_count, inner_width)
    partial_value = jnp.dot(
        gathered.reshape(rows_dev * grid_width, inner_width),
        output_proj,
        preferred_element_type=jnp.float32,
    )
    summed = lax.psum_scatter(
        partial_value.reshape(rows_dev, grid_width, -1).astype(jnp.bfloat16),
        "sub",
        scatter_dimension=2,
        tiled=True,
    )
    blended = latents.astype(jnp.float32) + gate_row * summed.astype(jnp.float32)
    return blended.astype(jnp.bfloat16)


LANES = 128
TOKEN_LIMIT = 256
LOG2_E = math.log2(math.e)


def hops(lines):
    count = lines.bit_length() - 1
    return [1 << i for i in sorted(range(count), key=lambda i: (i != count - 1, i))]


def swap_cores(tensor):
    return lax.ppermute(tensor, "sub", [(0, 1), (1, 0)])


def silu(values):
    half = 0.5 * values
    return half + half * jnp.tanh(half)


def softplus(values):
    return jnp.maximum(values, 0.0) + jnp.log(1.0 + jnp.exp(-jnp.abs(values)))


def matmul(left, right):
    return jnp.dot(left, right, preferred_element_type=jnp.float32)


def rounded(values):
    return values.astype(jnp.bfloat16).astype(jnp.float32)


def fetch_kernel(
    sel_ref,
    step_ref,
    mod_ref,
    into_ref,
    conv_ref,
    decay_ref,
    bias_ref,
    stepb_ref,
    skip_ref,
    latent_ref,
    out_ref,
    narrow_ref,
    wide_ref,
    held_ref,
    own_ref,
    send_ref,
    conv_buf,
    decay_buf,
    vector_bufs,
    sems,
):
    coefs, rank, taps = sel_ref.shape[0], step_ref.shape[0], conv_ref.shape[0]
    half = mod_ref.shape[-1]
    vectors = (bias_ref, stepb_ref, skip_ref)
    moves = [
        (conv_ref, conv_buf),
        (decay_ref, decay_buf),
        *((ref, vector_bufs[i]) for i, ref in enumerate(vectors)),
        (sel_ref, narrow_ref.at[:coefs]),
        (step_ref, narrow_ref.at[coefs : coefs + rank]),
        (mod_ref.at[0], narrow_ref.at[coefs + rank :, :half]),
        (mod_ref.at[1], narrow_ref.at[coefs + rank :, half:]),
        (latent_ref, own_ref),
        (out_ref.at[:, pl.ds(pl.multiple_of((1 - lax.axis_index("sub")) * half, LANES), half)], send_ref),
        (into_ref.at[: held_ref.shape[0]], held_ref),
    ]
    copies = [pltpu.make_async_copy(src, dst, sems.at[i]) for i, (src, dst) in enumerate(moves)]
    for copy in copies:
        copy.start()
    for copy in copies[: 2 + len(vectors)]:
        copy.wait()
    wide_ref[:taps] = conv_buf[...]
    for i, buf in enumerate(vector_bufs):
        wide_ref[taps + i : taps + i + 1] = buf[...].reshape(1, buf.shape[0])
    wide_ref[taps + 3 : taps + 4] = jnp.zeros((1, wide_ref.shape[1]), jnp.float32)
    wide_ref[taps + 4 :] = -LOG2_E * jnp.exp(decay_buf[...])
    for copy in copies[2 + len(vectors) :]:
        copy.wait()


def prepare_kernel(lead, order_ref, frequency_ref, mod_ref, narrow_ref, pick_ref, live_ref, rows_ref):
    height = order_ref.shape[0] - 1
    tokens = pick_ref.shape[1]
    width, half = tokens // height, mod_ref.shape[-1]
    own_row = lax.axis_index("rows") * lax.axis_size("cols") + lax.axis_index("cols")
    position = jnp.int32(0)
    for k in range(height):
        position = jnp.where(order_ref[k] == own_row, k, position)
    core = lax.axis_index("sub")
    slot = lax.broadcasted_iota(jnp.int32, (width, 2 * tokens), 0)
    column = lax.broadcasted_iota(jnp.int32, (width, 2 * tokens), 1)
    halves = ([], [])
    for j in range(height):
        away = order_ref[jnp.maximum(position - j, 0)] ^ own_row
        side, block = core, jnp.int32(0)
        for hop, reach in enumerate(hops(height)):
            crossed = (away // reach) & 1
            side, block = side ^ crossed, block + (crossed << hop)
        for part in range(2):
            start = (block + (side ^ part) * height) * width
            target = jnp.where(position >= j, start, -width) + slot
            halves[part].append(jnp.where(column == target, 1.0, 0.0))
        live_ref[j * width : (j + 1) * width] = jnp.full((width, LANES), jnp.where(position >= j, 1.0, 0.0))
    for part in range(2):
        pick_ref[part] = jnp.concatenate(halves[part], axis=0).astype(jnp.bfloat16)
    moment = jnp.full(frequency_ref.shape, order_ref[height]).astype(jnp.float32)
    angles = jnp.broadcast_to(moment * frequency_ref[...], (16, frequency_ref.shape[1]))
    embed = jnp.concatenate([jnp.cos(angles), jnp.sin(angles)], axis=1).astype(jnp.bfloat16)

    def mod_row(weight):
        return rounded(matmul(embed, weight))[:1]

    for i in range(2):
        mine, other = mod_row(mod_ref[i]), mod_row(narrow_ref[lead:, i * half : (i + 1) * half])
        for part in range(2):
            row = jnp.where(core == part, mine, other)
            rows_ref[2 * i + part : 2 * i + part + 1] = row if i else 1.0 + row
    rows_ref[4:5] = mod_row(mod_ref[2])


def block_kernel(
    taps,
    states,
    rank,
    pick_ref,
    live_ref,
    rows_ref,
    mine_ref,
    other_ref,
    in_mine,
    in_other,
    narrow_mine,
    narrow_other,
    wide_mine,
    wide_other,
    out_mine,
    out_other,
    result_ref,
    act_ref,
    pre_ref,
    weight_ref,
):
    height, width, half = mine_ref.shape
    tokens = height * width
    inner = in_mine.shape[-1]
    core = lax.axis_index("sub")
    coefs = rank + 2 * states
    gate_row = rows_ref[4:5]

    gathered = jnp.concatenate([ref[...].reshape(tokens, half) for ref in (mine_ref, other_ref)], axis=0)
    halves = [matmul(pick_ref[part], gathered) for part in range(2)]
    total = jnp.sum(halves[0] * halves[0] + halves[1] * halves[1], axis=-1, keepdims=True)
    scaling = lax.rsqrt(total / (2.0 * half) + EPSILON)
    live = live_ref[...]
    live_half = jnp.concatenate([live] * (half // LANES), axis=1)
    normed = jnp.concatenate(
        [
            (halves[part] * scaling * rows_ref[part : part + 1] + rows_ref[part + 2 : part + 3]) * live_half
            for part in range(2)
        ],
        axis=1,
    ).astype(jnp.bfloat16)
    own_normed = normed[:width]

    sides = ((in_mine, narrow_mine, wide_mine, out_mine), (in_other, narrow_other, wide_other, out_other))
    selected = None
    for side, (in_ref, narrow, wide, _) in enumerate(sides):
        seq = rounded(matmul(normed, in_ref[0]))
        pieces = []
        for j in range(height):
            mixed = wide[taps : taps + 1, :]
            for back in range(min(taps, height - j)):
                tap = taps - 1 - back
                mixed = mixed + wide[tap : tap + 1, :] * seq[(j + back) * width : (j + back + 1) * width]
            pieces.append(silu(mixed))
        act = jnp.concatenate(pieces, axis=0).astype(jnp.bfloat16)
        act_ref[side] = act.astype(jnp.float32)
        part = lax.dot_general(
            act, narrow[:coefs, :], (((1,), (1,)), ((), ())), preferred_element_type=jnp.float32
        )
        selected = part if selected is None else selected + part

    low_rank = selected[:, :rank].astype(jnp.bfloat16)
    for side, (_, narrow, _, _) in enumerate(sides):
        pre_ref[side] = matmul(low_rank, narrow[coefs : coefs + rank, :])
    own_exit = selected[:width, rank + states :]
    own_product = selected[:width, rank : rank + states] * own_exit
    latest = jnp.broadcast_to(jnp.sum(own_product, axis=1, keepdims=True), (width, LANES))
    for j in range(1, height):
        product = selected[j * width : (j + 1) * width, rank : rank + states] * own_exit
        product = product * live[j * width : (j + 1) * width, :states]
        for n in range(states):
            weight_ref[j, n] = jnp.broadcast_to(product[:, n : n + 1], (width, LANES))

    update = None
    columns = pl.ds(pl.multiple_of(core * half, LANES), half)
    for side, (in_ref, _, wide, out_ref) in enumerate(sides):
        gate = silu(rounded(matmul(own_normed, in_ref[1])))
        rates = wide[taps + 4 :, :]
        step_bias, skip = wide[taps + 1 : taps + 2, :], wide[taps + 2 : taps + 3, :]
        outs = []
        for block in range(inner // LANES):
            lanes = slice(block * LANES, (block + 1) * LANES)
            size = softplus(pre_ref[side, :, lanes] + step_bias[:, lanes])
            act = act_ref[side, :, lanes]
            drive = size * act
            rate = [jnp.broadcast_to(rates[n : n + 1, lanes], (width, LANES)) for n in range(states)]
            scanned = skip[:, lanes] * act[:width] + drive[:width] * latest
            elapsed = size[:width]
            for j in range(1, height):
                rows = slice(j * width, (j + 1) * width)
                mixed = None
                for n in range(states):
                    term = jnp.exp2(elapsed * rate[n]) * weight_ref[j, n]
                    mixed = term if mixed is None else mixed + term
                scanned = scanned + drive[rows] * mixed
                elapsed = elapsed + size[rows]
            outs.append((scanned * gate[:, lanes]).astype(jnp.bfloat16))
        part = matmul(jnp.concatenate(outs, axis=1), out_ref[...] if side else out_ref[:, columns])
        update = part if update is None else update + part
    own_latent = mine_ref[0].astype(jnp.float32)
    result_ref[...] = (own_latent + gate_row * rounded(update)).astype(jnp.bfloat16)


def gather_device(
    latents,
    timestep,
    scan_order,
    modulation,
    input_proj,
    conv_weight,
    conv_bias,
    select_proj,
    step_proj,
    step_bias,
    decay_log,
    skip_gain,
    output_proj,
):
    _, width, half = latents.shape
    lines = lax.axis_size(("rows", "cols"))
    inner, states = input_proj.shape[-1], decay_log.shape[0]
    taps, rank = conv_weight.shape[0], step_proj.shape[0]
    tokens = lines * width
    freq_count = modulation.shape[0]
    vmem = pl.BlockSpec(memory_space=pltpu.VMEM)
    smem = pl.BlockSpec(memory_space=pltpu.SMEM)
    by_row = modulation.transpose(1, 0, 2)
    coefs = select_proj.shape[1]
    cut = input_proj.shape[0] // 3 if input_proj.shape[0] % 3 == 0 else input_proj.shape[0] // 2
    halfway = freq_count // 2
    frequency = jnp.exp(-math.log(10000.0) * jnp.arange(halfway, dtype=jnp.float32) / halfway)[None]
    anywhere = pl.BlockSpec(memory_space=pl.ANY)
    narrow, wide, held, own, out_send = pl.pallas_call(
        fetch_kernel,
        out_shape=(
            jax.ShapeDtypeStruct((coefs + rank + freq_count, inner), jnp.bfloat16),
            jax.ShapeDtypeStruct((taps + 4 + states, inner), jnp.float32),
            jax.ShapeDtypeStruct((cut,) + input_proj.shape[1:], jnp.bfloat16),
            jax.ShapeDtypeStruct(latents.shape, jnp.bfloat16),
            jax.ShapeDtypeStruct((inner, half), jnp.bfloat16),
        ),
        in_specs=[anywhere] * 11,
        out_specs=[vmem] * 5,
        scratch_shapes=[
            pltpu.VMEM(conv_weight.shape, jnp.float32),
            pltpu.VMEM(decay_log.shape, jnp.float32),
            [pltpu.VMEM(conv_bias.shape, jnp.float32)] * 3,
            pltpu.SemaphoreType.DMA((12,)),
        ],
        compiler_params=pltpu.CompilerParams(vmem_limit_bytes=8 << 20),
        name="fetch",
    )(
        *(
            pltpu.with_memory_space_constraint(tensor, pltpu.HBM)
            for tensor in (
                select_proj.T,
                step_proj,
                by_row,
                input_proj,
                conv_weight,
                decay_log,
                conv_bias,
                step_bias,
                skip_gain,
                latents,
                output_proj,
            )
        )
    )
    gathered = latents
    out_other = swap_cores(out_send)
    for hop, reach in enumerate(hops(lines)):
        pairs = [(i, i ^ (2 * reach + 1)) for i in range(2 * lines)]
        arrived = lax.ppermute(gathered, ("rows", "cols", "sub"), pairs)
        gathered = jnp.concatenate([gathered if hop else own, arrived], 0)
    other = swap_cores(gathered)
    rest = input_proj[cut:].transpose(1, 0, 2)
    into = jnp.concatenate([held.transpose(1, 0, 2), rest], axis=1)
    into_other = swap_cores(into)
    narrow_other = swap_cores(narrow)
    wide_other = swap_cores(wide)
    scalars = jnp.concatenate([scan_order, timestep])
    pick, live, rows = pl.pallas_call(
        functools.partial(prepare_kernel, coefs + rank),
        out_shape=(
            jax.ShapeDtypeStruct((2, tokens, 2 * tokens), jnp.bfloat16),
            jax.ShapeDtypeStruct((tokens, LANES), jnp.float32),
            jax.ShapeDtypeStruct((8, half), jnp.float32),
        ),
        in_specs=[smem, vmem, vmem, vmem],
        out_specs=(vmem, vmem, vmem),
        compiler_params=pltpu.CompilerParams(vmem_limit_bytes=8 << 20),
        name="prepare",
    )(scalars, frequency, by_row, narrow_other)
    operands = (
        pick,
        live,
        rows,
        gathered,
        other,
        into,
        into_other,
        narrow,
        narrow_other,
        wide,
        wide_other,
        output_proj,
        out_other,
    )
    result = pl.pallas_call(
        functools.partial(block_kernel, taps, states, rank),
        out_shape=jax.ShapeDtypeStruct((width, half), jnp.bfloat16),
        in_specs=[vmem] * len(operands),
        out_specs=vmem,
        scratch_shapes=[
            pltpu.VMEM((2, tokens, inner), jnp.float32),
            pltpu.VMEM((2, tokens, inner), jnp.float32),
            pltpu.VMEM((lines, states, width, LANES), jnp.float32),
        ],
        compiler_params=pltpu.CompilerParams(vmem_limit_bytes=16 << 20),
        name="scan_block",
    )(*operands)
    return result[None]


def on_device(latents, *others):
    rows_dev, grid_width, half = latents.shape
    lines = lax.axis_size(("rows", "cols"))
    small = rows_dev == 1 and lines & (lines - 1) == 0 and lines * grid_width <= TOKEN_LIMIT
    tiled = grid_width % 8 == 0 and half % LANES == 0 and lax.axis_size("sub") == 2
    run = gather_device if small and tiled else exchange_device
    return run(latents, *others)


def solution(mesh):
    placed = (
        P(("groups", "rows", "cols"), None, "sub"),
        P("groups"),
        P(),
        P(None, None, "sub"),
        P(None, None, "sub"),
        P(None, "sub"),
        P("sub"),
        P("sub", None),
        P(None, "sub"),
        P("sub"),
        P(None, "sub"),
        P("sub"),
        P("sub", None),
    )
    return jax.shard_map(
        on_device,
        mesh=mesh,
        in_specs=placed,
        out_specs=P(("groups", "rows", "cols"), None, "sub"),
        check_vma=False,
    )
```

```python
import functools
import math

import jax
import jax.numpy as jnp
from jax import lax
from jax.experimental import pallas as pl
from jax.experimental.pallas import tpu as pltpu
from jax.sharding import PartitionSpec as P


NS = 16
RANK = 48


EPSILON = 1e-06


def embed_time(timestep, freq_count):
    halfway = freq_count // 2
    frequency = jnp.exp(-math.log(10000.0) * jnp.arange(halfway, dtype=jnp.float32) / halfway)
    angles = timestep.astype(jnp.float32)[0] * frequency
    return jnp.concatenate([jnp.cos(angles), jnp.sin(angles)]).astype(jnp.bfloat16)


def widen(latent_half, scale_shift):
    return (
        lax.all_gather(latent_half, "sub", axis=2, tiled=True),
        lax.all_gather(scale_shift, "sub", axis=1, tiled=True),
    )


def normalize(latent_full, scale_full):
    values = latent_full.astype(jnp.float32)
    meansq = jnp.mean(values * values, axis=-1, keepdims=True)
    scaled = values * lax.rsqrt(meansq + EPSILON)
    scale_row = scale_full[0].astype(jnp.float32)
    shift_row = scale_full[1].astype(jnp.float32)
    return (scaled * (1.0 + scale_row) + shift_row).astype(jnp.bfloat16)


def project_in(normed, input_proj):
    model_width = input_proj.shape[0]
    flat_weight = input_proj.reshape(model_width, -1)
    result = jnp.dot(
        normed.reshape(-1, model_width), flat_weight, preferred_element_type=jnp.float32
    )
    return result.astype(jnp.bfloat16).reshape(normed.shape[:-1] + (flat_weight.shape[1],))


def reorder(one_hot, sequence):
    return jnp.einsum("kh,hnc->knc", one_hot, sequence, preferred_element_type=jnp.float32).astype(
        jnp.bfloat16
    )


def restore(one_hot, sequence):
    return jnp.einsum("kh,knc->hnc", one_hot, sequence, preferred_element_type=jnp.float32).astype(
        jnp.bfloat16
    )


def scan_columns(
    projected, conv_weight, conv_bias, select_proj, step_proj, step_bias, decay_log, skip_gain
):
    height, item_count, doubled = projected.shape
    inner_width = doubled // 2
    seq_input = projected[..., :inner_width].astype(jnp.float32)
    seq_gate = projected[..., inner_width:].astype(jnp.float32)
    tap_count = conv_weight.shape[0]
    padded = jnp.pad(seq_input, ((tap_count - 1, 0), (0, 0), (0, 0)))
    conv_sum = conv_bias + jnp.zeros_like(seq_input)
    for offset in range(tap_count):
        conv_sum = conv_sum + conv_weight[offset] * padded[offset : offset + height]
    activated = jax.nn.silu(conv_sum).astype(jnp.bfloat16)
    flat_act = activated.reshape(height * item_count, inner_width)
    partial_value = lax.dot_general(
        select_proj, flat_act, (((0,), (1,)), ((), ())), preferred_element_type=jnp.float32
    )
    selected = lax.psum(partial_value, "sub")
    step_low = selected[:RANK].astype(jnp.bfloat16)
    step_pre = lax.dot_general(
        step_low, step_proj, (((0,), (0,)), ((), ())), preferred_element_type=jnp.float32
    )
    step_size = jax.nn.softplus(step_pre + step_bias).reshape(height, item_count, inner_width)
    entry_coef = selected[RANK : RANK + NS].T.reshape(height, item_count, NS)
    exit_coef = selected[RANK + NS :].T.reshape(height, item_count, NS)
    act_float = activated.astype(jnp.float32)
    decay_rate = -jnp.exp(decay_log)
    block_len = height // 16 if height % 16 == 0 else height
    blocks = height // block_len

    def split_blocks(tensor):
        return tensor.reshape((blocks, block_len) + tensor.shape[1:])

    def combine(earlier, latter):
        return (earlier[0] * latter[0], latter[0] * earlier[1] + latter[1])

    def advance(carried, pieces):
        step_blk, act_blk, entry_blk, exit_blk = pieces
        decays = jnp.exp(step_blk[:, :, None, :] * decay_rate)
        driving = (step_blk * act_blk)[:, :, None, :] * entry_blk[..., None]
        cum_decay, cum_drive = lax.associative_scan(combine, (decays, driving), axis=0)
        states = cum_drive + cum_decay * carried[None]
        output = jnp.sum(exit_blk[..., None] * states, axis=2) + skip_gain * act_blk
        return (states[-1], output)

    initial = jnp.zeros((item_count, NS, inner_width), jnp.float32)
    pieces_all = (
        split_blocks(step_size),
        split_blocks(act_float),
        split_blocks(entry_coef),
        split_blocks(exit_coef),
    )
    _, outputs = lax.scan(advance, initial, pieces_all)
    scanned = outputs.reshape(height, item_count, inner_width)
    return (scanned * jax.nn.silu(seq_gate)).astype(jnp.bfloat16)


def exchange_device(
    latents,
    timestep,
    scan_order,
    modulation,
    input_proj,
    conv_weight,
    conv_bias,
    select_proj,
    step_proj,
    step_bias,
    decay_log,
    skip_gain,
    output_proj,
):
    rows_dev, grid_width, half_model = latents.shape
    line_groups = lax.axis_size(("rows", "cols"))
    cols_dev = grid_width // line_groups
    height = rows_dev * line_groups
    inner_width = input_proj.shape[2]
    freq_count = modulation.shape[0]
    time_embed = embed_time(timestep, freq_count)
    mod_rows = jnp.dot(
        time_embed[None, :], modulation.reshape(freq_count, -1), preferred_element_type=jnp.float32
    )
    mod_rows = mod_rows.reshape(3, half_model).astype(jnp.bfloat16)
    scale_shift = mod_rows[:2]
    gate_row = mod_rows[2].astype(jnp.float32)
    one_hot = (scan_order[:, None] == jnp.arange(height, dtype=jnp.int32)[None, :]).astype(
        jnp.bfloat16
    )
    latent_full, scale_full = widen(latents, scale_shift)
    projected = project_in(normalize(latent_full, scale_full), input_proj)
    sectioned = projected.reshape(rows_dev, line_groups, cols_dev, 2 * inner_width)[None]
    received = lax.all_to_all(sectioned, ("rows", "cols"), split_axis=2, concat_axis=0, tiled=True)
    item_count = received.shape[3]
    ordered = reorder(one_hot, received.reshape(height, item_count, 2 * inner_width))
    gated = scan_columns(
        ordered, conv_weight, conv_bias, select_proj, step_proj, step_bias, decay_log, skip_gain
    )
    placed = restore(one_hot, gated)
    returned = lax.all_to_all(
        placed.reshape(line_groups, rows_dev, 1, item_count, inner_width),
        ("rows", "cols"),
        split_axis=0,
        concat_axis=2,
        tiled=True,
    )
    gathered = returned.reshape(rows_dev, line_groups, item_count, inner_width)
    partial_value = jnp.dot(
        gathered.reshape(rows_dev * grid_width, inner_width),
        output_proj,
        preferred_element_type=jnp.float32,
    )
    summed = lax.psum_scatter(
        partial_value.reshape(rows_dev, grid_width, -1).astype(jnp.bfloat16),
        "sub",
        scatter_dimension=2,
        tiled=True,
    )
    blended = latents.astype(jnp.float32) + gate_row * summed.astype(jnp.float32)
    return blended.astype(jnp.bfloat16)


LANES = 128
TOKEN_LIMIT = 256
LOG2_E = math.log2(math.e)


def hops(lines):
    count = lines.bit_length() - 1
    return [1 << i for i in sorted(range(count), key=lambda i: (i != count - 1, i))]


def swap_cores(tensor):
    return lax.ppermute(tensor, "sub", [(0, 1), (1, 0)])


def silu(values):
    half = 0.5 * values
    return half + half * jnp.tanh(half)


def softplus(values):
    return jnp.maximum(values, 0.0) + jnp.log(1.0 + jnp.exp(-jnp.abs(values)))


def matmul(left, right):
    return jnp.dot(left, right, preferred_element_type=jnp.float32)


def rounded(values):
    return values.astype(jnp.bfloat16).astype(jnp.float32)


def choose_rows(order_ref, pick_ref, live_ref):
    height = order_ref.shape[0]
    tokens = pick_ref.shape[1]
    width = tokens // height
    own_row = lax.axis_index("rows") * lax.axis_size("cols") + lax.axis_index("cols")
    core = lax.axis_index("sub")
    position = jnp.int32(0)
    for k in range(height):
        position = jnp.where(order_ref[k] == own_row, k, position)
    slot = lax.broadcasted_iota(jnp.int32, (width, 2 * tokens), 0)
    column = lax.broadcasted_iota(jnp.int32, (width, 2 * tokens), 1)
    halves = ([], [])
    for j in range(height):
        away = order_ref[jnp.maximum(position - j, 0)] ^ own_row
        side, block = core, jnp.int32(0)
        for hop, reach in enumerate(hops(height)):
            crossed = (away >> (reach.bit_length() - 1)) & 1
            side, block = side ^ crossed, block + (crossed << hop)
        for part in range(2):
            start = (block + (side ^ part) * height) * width
            target = jnp.where(position >= j, start, -width) + slot
            halves[part].append(jnp.where(column == target, 1.0, 0.0))
        live_ref[j * width : (j + 1) * width] = jnp.full((width, LANES), jnp.where(position >= j, 1.0, 0.0))
    for part in range(2):
        pick_ref[part] = jnp.concatenate(halves[part], axis=0).astype(jnp.bfloat16)


def fetch_kernel(
    sel_ref,
    step_ref,
    mod_ref,
    into_ref,
    conv_ref,
    decay_ref,
    bias_ref,
    stepb_ref,
    skip_ref,
    latent_ref,
    out_ref,
    order_ref,
    narrow_ref,
    wide_ref,
    held_ref,
    own_ref,
    send_ref,
    pick_ref,
    live_ref,
    order_buf,
    conv_buf,
    decay_buf,
    vector_bufs,
    sems,
):
    coefs, rank, taps = sel_ref.shape[0], step_ref.shape[0], conv_ref.shape[0]
    half = mod_ref.shape[-1]
    vectors = (bias_ref, stepb_ref, skip_ref)
    moves = [
        (order_ref, order_buf),
        (conv_ref, conv_buf),
        (decay_ref, decay_buf),
        *((ref, vector_bufs[i]) for i, ref in enumerate(vectors)),
        (sel_ref, narrow_ref.at[:coefs]),
        (step_ref, narrow_ref.at[coefs : coefs + rank]),
        (mod_ref.at[0], narrow_ref.at[coefs + rank :, :half]),
        (mod_ref.at[1], narrow_ref.at[coefs + rank :, half:]),
        (latent_ref, own_ref),
        (out_ref.at[:, pl.ds(pl.multiple_of((1 - lax.axis_index("sub")) * half, LANES), half)], send_ref),
        (into_ref.at[: held_ref.shape[0]], held_ref),
    ]
    copies = [pltpu.make_async_copy(src, dst, sems.at[i]) for i, (src, dst) in enumerate(moves)]
    for copy in copies:
        copy.start()
    for copy in copies[: 3 + len(vectors)]:
        copy.wait()
    wide_ref[:taps] = conv_buf[...]
    for i, buf in enumerate(vector_bufs):
        wide_ref[taps + i : taps + i + 1] = buf[...].reshape(1, buf.shape[0])
    wide_ref[taps + 3 : taps + 4] = jnp.zeros((1, wide_ref.shape[1]), jnp.float32)
    wide_ref[taps + 4 :] = -LOG2_E * jnp.exp(decay_buf[...])
    choose_rows(order_buf, pick_ref, live_ref)
    for copy in copies[3 + len(vectors) :]:
        copy.wait()


def prepare_kernel(lead, angle_ref, mod_ref, narrow_ref, rows_ref):
    half = mod_ref.shape[-1]
    core = lax.axis_index("sub")
    angles = jnp.broadcast_to(angle_ref[...], (16, angle_ref.shape[1]))
    embed = jnp.concatenate([jnp.cos(angles), jnp.sin(angles)], axis=1).astype(jnp.bfloat16)

    def mod_row(weight):
        return rounded(matmul(embed, weight))[:1]

    for i in range(2):
        mine, other = mod_row(mod_ref[i]), mod_row(narrow_ref[lead:, i * half : (i + 1) * half])
        for part in range(2):
            row = jnp.where(core == part, mine, other)
            rows_ref[2 * i + part : 2 * i + part + 1] = row if i else 1.0 + row
    rows_ref[4:5] = mod_row(mod_ref[2])


def block_kernel(
    taps,
    states,
    rank,
    pick_ref,
    live_ref,
    rows_ref,
    mine_ref,
    other_ref,
    in_mine,
    in_other,
    narrow_mine,
    narrow_other,
    wide_mine,
    wide_other,
    out_mine,
    out_other,
    result_ref,
    act_ref,
    pre_ref,
    weight_ref,
):
    height, width, half = mine_ref.shape
    tokens = height * width
    inner = in_mine.shape[-1]
    core = lax.axis_index("sub")
    coefs = rank + 2 * states
    gate_row = rows_ref[4:5]

    gathered = jnp.concatenate([ref[...].reshape(tokens, half) for ref in (mine_ref, other_ref)], axis=0)
    halves = [matmul(pick_ref[part], gathered) for part in range(2)]
    total = jnp.sum(halves[0] * halves[0] + halves[1] * halves[1], axis=-1, keepdims=True)
    scaling = lax.rsqrt(total / (2.0 * half) + EPSILON)
    live = live_ref[...]
    live_half = jnp.concatenate([live] * (half // LANES), axis=1)
    normed = jnp.concatenate(
        [
            (halves[part] * scaling * rows_ref[part : part + 1] + rows_ref[part + 2 : part + 3]) * live_half
            for part in range(2)
        ],
        axis=1,
    ).astype(jnp.bfloat16)
    own_normed = normed[:width]

    sides = ((in_mine, narrow_mine, wide_mine, out_mine), (in_other, narrow_other, wide_other, out_other))
    selected = None
    for side, (in_ref, narrow, wide, _) in enumerate(sides):
        seq = rounded(matmul(normed, in_ref[0]))
        pieces = []
        for j in range(height):
            mixed = wide[taps : taps + 1, :]
            for back in range(min(taps, height - j)):
                tap = taps - 1 - back
                mixed = mixed + wide[tap : tap + 1, :] * seq[(j + back) * width : (j + back + 1) * width]
            pieces.append(silu(mixed))
        act = jnp.concatenate(pieces, axis=0).astype(jnp.bfloat16)
        act_ref[side] = act.astype(jnp.float32)
        part = lax.dot_general(
            act, narrow[:coefs, :], (((1,), (1,)), ((), ())), preferred_element_type=jnp.float32
        )
        selected = part if selected is None else selected + part

    low_rank = selected[:, :rank].astype(jnp.bfloat16)
    for side, (_, narrow, _, _) in enumerate(sides):
        pre_ref[side] = matmul(low_rank, narrow[coefs : coefs + rank, :])
    own_exit = selected[:width, rank + states :]
    own_product = selected[:width, rank : rank + states] * own_exit
    latest = jnp.broadcast_to(jnp.sum(own_product, axis=1, keepdims=True), (width, LANES))
    for j in range(1, height):
        product = selected[j * width : (j + 1) * width, rank : rank + states] * own_exit
        product = product * live[j * width : (j + 1) * width, :states]
        for n in range(states):
            weight_ref[j, n] = jnp.broadcast_to(product[:, n : n + 1], (width, LANES))

    update = None
    columns = pl.ds(pl.multiple_of(core * half, LANES), half)
    for side, (in_ref, _, wide, out_ref) in enumerate(sides):
        gate = silu(rounded(matmul(own_normed, in_ref[1])))
        rates = wide[taps + 4 :, :]
        step_bias, skip = wide[taps + 1 : taps + 2, :], wide[taps + 2 : taps + 3, :]
        outs = []
        for block in range(inner // LANES):
            lanes = slice(block * LANES, (block + 1) * LANES)
            size = softplus(pre_ref[side, :, lanes] + step_bias[:, lanes])
            act = act_ref[side, :, lanes]
            drive = size * act
            rate = [jnp.broadcast_to(rates[n : n + 1, lanes], (width, LANES)) for n in range(states)]
            scanned = skip[:, lanes] * act[:width] + drive[:width] * latest
            elapsed = size[:width]
            for j in range(1, height):
                rows = slice(j * width, (j + 1) * width)
                mixed = None
                for n in range(states):
                    term = jnp.exp2(elapsed * rate[n]) * weight_ref[j, n]
                    mixed = term if mixed is None else mixed + term
                scanned = scanned + drive[rows] * mixed
                elapsed = elapsed + size[rows]
            outs.append((scanned * gate[:, lanes]).astype(jnp.bfloat16))
        part = matmul(jnp.concatenate(outs, axis=1), out_ref[...] if side else out_ref[:, columns])
        update = part if update is None else update + part
    own_latent = mine_ref[0].astype(jnp.float32)
    result_ref[...] = (own_latent + gate_row * rounded(update)).astype(jnp.bfloat16)


def gather_device(
    latents,
    timestep,
    scan_order,
    modulation,
    input_proj,
    conv_weight,
    conv_bias,
    select_proj,
    step_proj,
    step_bias,
    decay_log,
    skip_gain,
    output_proj,
):
    _, width, half = latents.shape
    lines = lax.axis_size(("rows", "cols"))
    inner, states = input_proj.shape[-1], decay_log.shape[0]
    taps, rank = conv_weight.shape[0], step_proj.shape[0]
    tokens = lines * width
    freq_count = modulation.shape[0]
    vmem = pl.BlockSpec(memory_space=pltpu.VMEM)
    by_row = modulation.transpose(1, 0, 2)
    coefs = select_proj.shape[1]
    cut = input_proj.shape[0] // 3 if input_proj.shape[0] % 3 == 0 else input_proj.shape[0] // 2
    anywhere = pl.BlockSpec(memory_space=pl.ANY)
    narrow, wide, held, own, out_send, pick, live = pl.pallas_call(
        fetch_kernel,
        out_shape=(
            jax.ShapeDtypeStruct((coefs + rank + freq_count, inner), jnp.bfloat16),
            jax.ShapeDtypeStruct((taps + 4 + states, inner), jnp.float32),
            jax.ShapeDtypeStruct((cut,) + input_proj.shape[1:], jnp.bfloat16),
            jax.ShapeDtypeStruct(latents.shape, jnp.bfloat16),
            jax.ShapeDtypeStruct((inner, half), jnp.bfloat16),
            jax.ShapeDtypeStruct((2, tokens, 2 * tokens), jnp.bfloat16),
            jax.ShapeDtypeStruct((tokens, LANES), jnp.float32),
        ),
        in_specs=[anywhere] * 12,
        out_specs=[vmem] * 7,
        scratch_shapes=[
            pltpu.SMEM(scan_order.shape, jnp.int32),
            pltpu.VMEM(conv_weight.shape, jnp.float32),
            pltpu.VMEM(decay_log.shape, jnp.float32),
            [pltpu.VMEM(conv_bias.shape, jnp.float32)] * 3,
            pltpu.SemaphoreType.DMA((13,)),
        ],
        compiler_params=pltpu.CompilerParams(vmem_limit_bytes=8 << 20),
        name="fetch",
    )(
        *(
            pltpu.with_memory_space_constraint(tensor, pltpu.HBM)
            for tensor in (
                select_proj.T,
                step_proj,
                by_row,
                input_proj,
                conv_weight,
                decay_log,
                conv_bias,
                step_bias,
                skip_gain,
                latents,
                output_proj,
                scan_order,
            )
        )
    )
    gathered = latents
    out_other = swap_cores(out_send)
    for hop, reach in enumerate(hops(lines)):
        pairs = [(i, i ^ (2 * reach + 1)) for i in range(2 * lines)]
        arrived = lax.ppermute(gathered, ("rows", "cols", "sub"), pairs)
        gathered = jnp.concatenate([gathered if hop else own, arrived], 0)
    other = swap_cores(gathered)
    rest = input_proj[cut:].transpose(1, 0, 2)
    into = jnp.concatenate([held.transpose(1, 0, 2), rest], axis=1)
    into_other = swap_cores(into)
    narrow_other = swap_cores(narrow)
    wide_other = swap_cores(wide)
    halfway = freq_count // 2
    frequency = jnp.exp(-math.log(10000.0) * jnp.arange(halfway, dtype=jnp.float32) / halfway)
    angles = timestep.astype(jnp.float32)[:, None] * frequency[None]
    rows = pl.pallas_call(
        functools.partial(prepare_kernel, coefs + rank),
        out_shape=jax.ShapeDtypeStruct((8, half), jnp.float32),
        in_specs=[vmem, vmem, vmem],
        out_specs=vmem,
        compiler_params=pltpu.CompilerParams(vmem_limit_bytes=8 << 20),
        name="prepare",
    )(angles, by_row, narrow_other)
    operands = (
        pick,
        live,
        rows,
        gathered,
        other,
        into,
        into_other,
        narrow,
        narrow_other,
        wide,
        wide_other,
        output_proj,
        out_other,
    )
    result = pl.pallas_call(
        functools.partial(block_kernel, taps, states, rank),
        out_shape=jax.ShapeDtypeStruct((width, half), jnp.bfloat16),
        in_specs=[vmem] * len(operands),
        out_specs=vmem,
        scratch_shapes=[
            pltpu.VMEM((2, tokens, inner), jnp.float32),
            pltpu.VMEM((2, tokens, inner), jnp.float32),
            pltpu.VMEM((lines, states, width, LANES), jnp.float32),
        ],
        compiler_params=pltpu.CompilerParams(vmem_limit_bytes=16 << 20),
        name="scan_block",
    )(*operands)
    return result[None]


def on_device(latents, *others):
    rows_dev, grid_width, half = latents.shape
    lines = lax.axis_size(("rows", "cols"))
    small = rows_dev == 1 and lines & (lines - 1) == 0 and lines * grid_width <= TOKEN_LIMIT
    tiled = grid_width % 8 == 0 and half % LANES == 0 and lax.axis_size("sub") == 2
    run = gather_device if small and tiled else exchange_device
    return run(latents, *others)


def solution(mesh):
    placed = (
        P(("groups", "rows", "cols"), None, "sub"),
        P("groups"),
        P(),
        P(None, None, "sub"),
        P(None, None, "sub"),
        P(None, "sub"),
        P("sub"),
        P("sub", None),
        P(None, "sub"),
        P("sub"),
        P(None, "sub"),
        P("sub"),
        P("sub", None),
    )
    return jax.shard_map(
        on_device,
        mesh=mesh,
        in_specs=placed,
        out_specs=P(("groups", "rows", "cols"), None, "sub"),
        check_vma=False,
    )
```
